512 devices in a mesh: group: 16 (over y_lo, x, core), mp: 32 (over z, y_hi).
Axes of the slice: x: 4, y: 4 (y_hi: 2, y_lo: 2; y = y_hi * 2 + y_lo), z: 16, core: 2. Of those that a mesh axis runs over, the one named last changes fastest.
Arguments:
- arrivals: bfloat16 [65536, 2048], P(('group', 'mp')), may hold values from -6 to 6
- slots: int32 [65536], P(('group', 'mp')), may hold values from 0 to 4095, as said below
- lengths: int32 [16, 4], P('group'), may hold values from 1 to 3072, 4096 in all within a row
- w_joined: float32 [2048, 1536], P('mp', 'group')
- w_expand: float32 [512, 2048], P('mp', 'group'), may hold values from -0.25 to 0.25
Outputs:
- attended: bfloat16 [65536, 1024], P(('group', 'mp'))
The draws below stay inside these ranges and needn't reach their ends.
Inputs may be any that keep to these rules, and one draw needn't show every extreme that they name: `slots`: within each group the entries form a permutation of 0 to 4095; the 128 entries of one device hold exactly 2 values of every aligned run of 64 values.
All inputs are finite; a program needn't handle non-finite values.
Results may differ from the reference program's by a relative error of at most 0.03.
The reference program's roundings to bfloat16 on the way (of `served`, `normed`, `query`, `latent`, `keyval`, `probs` and `outcome`) count: a program that leaves them out, or rounds other values in their place, can miss the bound.
Values may be sent and summed in bfloat16 or wider, within the bound.
A program may use at most 64 MiB of HBM per device.

```python
import math
import jax
import jax.numpy as jnp
import numpy as np
from jax import lax

D = 2048
HEADS = 8
HDIM = 128
RANK = 512
TOK_DEV = 128
QCOLS = 1024
JOINED = 1536
TOKG = 4096
TOKENS = 65536
COUNT = 4
N_GROUP = 16
N_MP = 32


def draw_slots(key, part):
    group_tokens = TOK_DEV * N_MP
    half_rows = TOK_DEV // 2
    per_block = half_rows // N_MP
    block_count = 2 * N_MP

    def one_group(group_key):
        block_key = jax.random.fold_in(group_key, 1)
        shuffle_key = jax.random.fold_in(group_key, 2)
        block_perms = jax.vmap(lambda one_key: jax.random.permutation(one_key, half_rows))(jax.random.split(block_key, block_count))
        block_perms = block_perms.astype(jnp.int32) + (jnp.arange(block_count, dtype=jnp.int32) * half_rows)[:, None]
        grouped = jnp.transpose(block_perms.reshape(block_count, N_MP, per_block), (1, 0, 2)).reshape(N_MP, TOK_DEV)
        shuffles = jax.vmap(lambda one_key: jax.random.permutation(one_key, TOK_DEV))(jax.random.split(shuffle_key, N_MP))
        return jnp.take_along_axis(grouped, shuffles.astype(jnp.int32), axis=1).reshape(group_tokens)
    group_keys = jax.random.split(jax.random.fold_in(key, 11), N_GROUP)
    return jax.vmap(one_group)(group_keys).reshape(N_GROUP * group_tokens).astype(jnp.int32)


def draw_w_joined(key, part):
    values = jax.random.normal(jax.random.fold_in(key, 3), (D, JOINED), jnp.float32) * D ** (-0.5)
    return values


def steps_of(key, shape, cuts, least, largest):
    factor_of, own = 1.0, jax.random.fold_in(key, 6)
    for dim, parts in cuts:
        steps = jnp.exp(jax.random.uniform(jax.random.fold_in(own, dim), (parts,), jnp.float32, least / len(cuts), largest / len(cuts)))
        factor_of = factor_of * jnp.repeat(steps, shape[dim] // parts).reshape([-1 if axis == dim else 1 for axis in range(len(shape))])
    return factor_of


def split_up(count, total, limit, skew):
    portions = [(1 << 20) // math.isqrt(grade ** skew) + 1 for grade in range(2, count + 1)]
    surplus, counts = total - limit - (count - 1), [1] * (count - 1)
    while surplus > 0:
        free = [i for i in range(count - 1) if counts[i] < limit]
        whole, remaining = sum([portions[i] for i in free]), surplus
        for i in free:
            more = min(limit - counts[i], max(1, remaining * portions[i] // whole), surplus)
            counts[i] = counts[i] + more
            surplus = surplus - more
    return np.array([limit] + counts)


def ragged(own_key, count, total, reach, slope):
    if count == 2:
        one = jax.random.randint(own_key, (), max(1, total - reach), min(reach, total - 1) + 1)
        return jnp.stack([one, total - one])
    sizes = jnp.asarray(split_up(count, total, reach, slope), jnp.int32)
    twos = (count - 1) // 2
    giver, sink = sizes[1:1 + 2 * twos:2], sizes[2:2 + 2 * twos:2]
    margin = jnp.minimum(giver - 1, reach - sink)
    moved = jax.random.randint(jax.random.fold_in(own_key, 1), (twos,), 0, 1 << 20) % (margin + 1)
    sizes = sizes.at[1:1 + 2 * twos:2].set(giver - moved).at[2:2 + 2 * twos:2].set(sink + moved)
    return sizes[jax.random.permutation(jax.random.fold_in(own_key, 2), count)]


def normal_values(rng, extent, deviation, reach, cuts=(), kind=jnp.bfloat16):
    loudness = steps_of(rng, extent, cuts, -0.22, 0.18) if cuts else 1.0
    values = jax.random.normal(rng, extent, jnp.float32) * deviation * loudness
    return jnp.minimum(jnp.maximum(values, -reach), reach).astype(kind)


def setup_inputs(seed: int = 0) -> dict:
    streams_of = jax.random.split(jax.random.key(seed), 6)
    return {
        "arrivals": normal_values(streams_of[0], (TOKENS, D), 1.0, 6.0, ((0, 512),)),
        "slots": draw_slots(jax.random.fold_in(streams_of[5], 71), 0),
        "lengths": jax.vmap(lambda own: ragged(own, COUNT, TOKG, 3 * TOKG // 4, 2))(jax.random.split(streams_of[2], N_GROUP)).reshape((N_GROUP, COUNT)).astype(jnp.int32),
        "w_joined": draw_w_joined(jax.random.fold_in(streams_of[5], 71), 0),
        "w_expand": normal_values(streams_of[4], (RANK, 2 * QCOLS), RANK ** -0.5, 0.25, ((0, 32), (1, 16)), jnp.float32),
    }


EPS = 1e-06
NEGATIVE = -1e+30

def row_norm(values):
    mean_sq = lax.optimization_barrier(jnp.mean(values * values, axis=-1, keepdims=True))
    return values * lax.rsqrt(mean_sq + EPS)

def reference(arrivals, slots, lengths, w_joined, w_expand):
    qcols = HEADS * HDIM
    joined_half = w_joined.astype(jnp.bfloat16)
    expand_half = w_expand.astype(jnp.bfloat16)
    group_rows = arrivals.reshape(N_GROUP, TOKG, D)
    group_slots = slots.reshape(N_GROUP, TOKG)
    block_rows = min(512, TOKG)
    window = min(TOKG, block_rows + 3 * TOKG // 4)

    def one_group(inputs):
        rows_in, slots_in, lengths_in = inputs
        served = jnp.zeros_like(rows_in).at[slots_in].set(rows_in)
        normed = row_norm(served.astype(jnp.float32)).astype(jnp.bfloat16)
        proj = jnp.dot(normed, joined_half, preferred_element_type=jnp.float32)
        query = (proj[:, :qcols] * HDIM ** (-0.5)).astype(jnp.bfloat16)
        latent = row_norm(proj[:, qcols:]).astype(jnp.bfloat16)
        keyval = jnp.dot(latent, expand_half, preferred_element_type=jnp.float32).astype(jnp.bfloat16)
        keyval = lax.optimization_barrier(keyval).reshape(TOKG, HEADS, 2 * HDIM)
        ends = jnp.cumsum(lengths_in).astype(jnp.int32)
        positions = jnp.arange(TOKG, dtype=jnp.int32)
        segment = lax.optimization_barrier(jnp.sum((positions[:, None] >= ends[None, :]).astype(jnp.int32), axis=1)).astype(jnp.int32)

        def one_block(block_index):
            first_row = (block_index * block_rows).astype(jnp.int32)
            key_first = jnp.clip(first_row + block_rows - window, 0, TOKG - window).astype(jnp.int32)
            queries = lax.dynamic_slice_in_dim(query, first_row, block_rows, 0)
            queries = queries.reshape(block_rows, HEADS, HDIM).astype(jnp.float32)
            key_rows = lax.dynamic_slice_in_dim(keyval, key_first, window, 0).astype(jnp.float32)
            scores = jnp.einsum('qhd,khd->hqk', queries, key_rows[:, :, :HDIM])
            query_pos = first_row + jnp.arange(block_rows, dtype=jnp.int32)
            key_pos = key_first + jnp.arange(window, dtype=jnp.int32)
            query_seg = lax.dynamic_slice_in_dim(segment, first_row, block_rows, 0)
            key_seg = lax.dynamic_slice_in_dim(segment, key_first, window, 0)
            allowed = (key_pos[None, :] <= query_pos[:, None]) & (key_seg[None, :] == query_seg[:, None])
            masked = jnp.where(allowed[None], scores, NEGATIVE)
            peak = lax.optimization_barrier(jnp.max(masked, axis=-1, keepdims=True))
            weights = jnp.where(allowed[None], jnp.exp(masked - peak), 0.0)
            total = lax.optimization_barrier(jnp.sum(weights, axis=-1))
            probs = lax.optimization_barrier(weights.astype(jnp.bfloat16)).astype(jnp.float32)
            summed = jnp.einsum('hqk,khd->qhd', probs, key_rows[:, :, HDIM:])
            return (summed / jnp.transpose(total)[:, :, None]).reshape(block_rows, qcols)
        outcome = lax.map(one_block, jnp.arange(TOKG // block_rows, dtype=jnp.int32))
        outcome = outcome.reshape(TOKG, qcols).astype(jnp.bfloat16)
        return outcome[slots_in]
    result = lax.map(one_group, (group_rows, group_slots, lengths))
    return result.reshape(TOKENS, qcols)
```

```python
import functools

import jax
import jax.numpy as jnp
from jax import lax
from jax.experimental import pallas as pl
from jax.experimental.pallas import tpu as pltpu
from jax.sharding import PartitionSpec as P

HEADS = 8
HDIM = 128
QCOLS = HEADS * HDIM
RANK = 512
WIDTH = 2048
ROWS = 128
NZ = 16
JPART = 384
BLOCK = 256
EPS = 1e-06
NEGATIVE = -1e30
OPEN = 3e38
MESH = pl.DeviceIdType.MESH
LAST = (((1,), (1,)), ((), ()))


def kernel(
    arrivals_ref,
    slot_row_ref,
    slot_col_ref,
    lengths_ref,
    joined_ref,
    expand_ref,
    out_ref,
    wide,
    quad,
    full,
    proj,
    lat,
    kpos,
    absorbed,
    peak,
    total,
    acc,
    q_send,
    q_recv,
    z_send,
    z_recv,
    kz_send,
    kz_recv,
    y_send,
    y_recv,
    ky_send,
    ky_recv,
    x_send,
    x_recv,
    c_send,
    c_recv,
    h_send,
    h_recv,
    r_send,
    r_recv,
):
    g = lax.axis_index("group")
    m = lax.axis_index("mp")
    core, x, ylo = g % 2, (g // 2) % 4, g // 8
    z, yhi = m // 2, m % 2
    xl, xh = x % 2, x // 2
    y = yhi * 2 + ylo

    def group_of(ylo_, x_, core_):
        return (ylo_ * 4 + x_) * 2 + core_

    def mp_of(z_, yhi_):
        return z_ * 2 + yhi_

    def flip(value, bits, span):
        if span == 2:
            return (value + bits) % 2
        if bits == 2:
            return (value + 2) % 4
        low = value % 2
        if bits == 1:
            return value + 1 - 2 * low
        return 3 - value

    def y_peer(k):
        other = flip(y, k, 4)
        return (group_of(other % 2, x, core), mp_of(z, other // 2))

    def x_peer(k):
        return (group_of(ylo, flip(x, k, 4), core), m)

    core_peer = (group_of(ylo, x, 1 - core), m)
    diag_peer = (group_of(ylo, flip(x, 1, 4), 1 - core), m)
    half_peer = (g, mp_of(z, 1 - yhi))
    right = (g, mp_of((z + 1) % NZ, yhi))
    left = (g, mp_of((z + NZ - 1) % NZ, yhi))

    barrier = pltpu.get_barrier_semaphore()

    def greet(peer):
        pl.semaphore_signal(barrier, inc=1, device_id=peer, device_id_type=MESH)

    @pl.loop(1, NZ)
    def _(dz):
        greet((g, mp_of((z + dz) % NZ, yhi)))

    for k in (1, 2, 3):
        greet(y_peer(k))
        greet(x_peer(k))
    greet(core_peer)
    greet(diag_peer)

    def remote(src, dst, send, recv, peer):
        return pltpu.make_async_remote_copy(
            src_ref=src,
            dst_ref=dst,
            send_sem=send,
            recv_sem=recv,
            device_id=peer,
            device_id_type=MESH,
        )

    my_r = xl * 2 + core
    row_id = lax.broadcasted_iota(jnp.int32, (96, JPART), 0)
    col_id = lax.broadcasted_iota(jnp.int32, (96, JPART), 1)
    place = jnp.where(col_id == row_id + my_r * 96, 1.0, 0.0).astype(jnp.bfloat16)
    wide[...] = (
        jnp.dot(joined_ref[...].astype(jnp.bfloat16), place, preferred_element_type=jnp.float32)
        .astype(jnp.bfloat16)
        .reshape(4, 16, JPART)
    )
    kpos[z, yhi] = jnp.broadcast_to(slot_row_ref[...], (8, ROWS))
    quad[my_r] = wide[my_r]

    pl.semaphore_wait(barrier, 23)

    def quad_copy(k):
        pxl, pcore = (xl + k // 2) % 2, (core + k % 2) % 2
        peer = (group_of(ylo, xh * 2 + pxl, pcore), m)
        return remote(
            wide.at[pxl * 2 + pcore], quad.at[my_r], q_send.at[k], q_recv.at[k], peer
        )

    def quad_arrival(k):
        pxl, pcore = (xl + k // 2) % 2, (core + k % 2) % 2
        slot = pxl * 2 + pcore
        return remote(quad.at[slot], quad.at[slot], q_send.at[k], q_recv.at[k], core_peer)

    for k in (1, 2, 3):
        quad_copy(k).start()

    @pl.loop(1, NZ)
    def _(dz):
        peer = (g, mp_of((z + dz) % NZ, yhi))
        remote(kpos.at[z, yhi], kpos.at[z, yhi], kz_send.at[dz], kz_recv.at[dz], peer).start()

    for k in (1, 2, 3):
        quad_arrival(k).wait_recv()
    pieces = quad[...].astype(jnp.float32)
    mine = full.at[ylo, xh, z, yhi, xl, core]
    mine[:, :JPART] = (pieces[0] + pieces[1] + pieces[2] + pieces[3]).astype(jnp.bfloat16)
    mine[:, JPART:] = expand_ref[...].astype(jnp.bfloat16)

    @pl.loop(1, NZ)
    def _(dz):
        peer = (g, mp_of((z + dz) % NZ, yhi))
        remote(mine, mine, z_send.at[dz], z_recv.at[dz], peer).start()

    values = arrivals_ref[...].astype(jnp.float32)
    mean_sq = jnp.mean(values * values, axis=-1, keepdims=True)
    normed = (values * lax.rsqrt(mean_sq + EPS)).astype(jnp.bfloat16)

    @pl.loop(1, NZ)
    def _(dz):
        source = (z + NZ - dz) % NZ
        slot = full.at[ylo, xh, source, yhi, xl, core]
        remote(slot, slot, z_send.at[dz], z_recv.at[dz], right).wait_recv()
        keys = kpos.at[source, yhi]
        remote(keys, keys, kz_send.at[dz], kz_recv.at[dz], right).wait_recv()

    def y_copy(ylo_, yhi_, k, peer):
        part = full.at[ylo_, xh, :, yhi_, xl, core]
        return remote(part, part, y_send.at[k], y_recv.at[k], peer)

    for k in (1, 2, 3):
        y_copy(ylo, yhi, k, y_peer(k)).start()
    key_copy = remote(kpos.at[:, yhi], kpos.at[:, yhi], ky_send, ky_recv, half_peer)
    key_copy.start()
    for k in (1, 2, 3):
        other = flip(y, k, 4)
        y_copy(other % 2, other // 2, k, core_peer).wait_recv()

    def x_copy(x_, k, peer):
        part = full.at[:, x_ // 2, :, :, x_ % 2, core]
        return remote(part, part, x_send.at[k], x_recv.at[k], peer)

    for k in (1, 2, 3):
        x_copy(x, k, x_peer(k)).start()
    for k in (1, 2, 3):
        x_copy(flip(x, k, 4), k, core_peer).wait_recv()

    def c_copy(core_):
        part = full.at[:, :, :, :, :, core_]
        return remote(part, part, c_send, c_recv, core_peer)

    c_copy(core).start()
    c_copy(1 - core).wait_recv()

    for c in range(4):
        weight = full[c // 2, c % 2, :, :, :, :, :, 0:JPART].reshape(WIDTH, JPART)
        proj[:, c * JPART : (c + 1) * JPART] = jnp.dot(
            normed, weight, preferred_element_type=jnp.float32
        )
    raw = proj[:, QCOLS:]
    raw_sq = jnp.mean(raw * raw, axis=-1, keepdims=True)
    lat[z, yhi] = (raw * lax.rsqrt(raw_sq + EPS)).astype(jnp.bfloat16)

    def half_copy(yhi_):
        return remote(lat.at[z, yhi_], lat.at[z, yhi_], h_send, h_recv, half_peer)

    def ring_send(way, step, half):
        source = (z + NZ - step) % NZ if way == 0 else (z + step) % NZ
        block = lat.at[source, half]
        peer = right if way == 0 else left
        return remote(
            block, block, r_send.at[way, step, half], r_recv.at[way, step, half], peer
        )

    def ring_arrival(way, step, half):
        source = (z + 2 * NZ - 1 - step) % NZ if way == 0 else (z + 1 + step) % NZ
        block = lat.at[source, half]
        return remote(
            block, block, r_send.at[way, step, half], r_recv.at[way, step, half], right
        )

    half_copy(yhi).start()
    ring_send(0, 0, yhi).start()
    ring_send(1, 0, yhi).start()

    def expand_block(index):
        ylo_, x_, core_ = index // 8, (index // 2) % 4, index % 2
        return full[ylo_, x_ // 2, :, :, x_ % 2, core_, :, JPART:].reshape(RANK, HDIM)

    for h in range(HEADS):
        query = (proj[:, h * HDIM : (h + 1) * HDIM] * HDIM ** (-0.5)).astype(jnp.bfloat16)
        absorbed[h * ROWS : (h + 1) * ROWS, :] = lax.dot_general(
            query, expand_block(2 * h), LAST, preferred_element_type=jnp.float32
        ).astype(jnp.bfloat16)

    half_copy(1 - yhi).wait_recv()
    ring_send(0, 0, 1 - yhi).start()
    ring_send(1, 0, 1 - yhi).start()
    remote(kpos.at[:, 1 - yhi], kpos.at[:, 1 - yhi], ky_send, ky_recv, half_peer).wait_recv()

    query_pos = slot_col_ref[...]
    first = jnp.zeros_like(query_pos)
    end = lengths_ref[0, 0]
    for p in range(1, 4):
        first = jnp.where(query_pos >= end, end, first)
        end = end + lengths_ref[0, p]

    def limit_of(source):
        keys = jnp.concatenate([kpos[source, 0][0:1], kpos[source, 1][0:1]], axis=1)
        allowed = (keys <= query_pos) & (keys >= first)
        return jnp.where(allowed, OPEN, NEGATIVE)

    def attend(sources, start):
        limits = [limit_of(source) for source in sources]

        @pl.loop(0, HEADS * ROWS // BLOCK)
        def _(block):
            rows = pl.ds(pl.multiple_of(block * BLOCK, BLOCK), BLOCK)
            query = absorbed[rows, :]
            keys = [lat[source].reshape(2 * ROWS, RANK) for source in sources]
            scores = []
            for key, limit in zip(keys, limits):
                score = lax.dot_general(query, key, LAST, preferred_element_type=jnp.float32)
                score = jnp.minimum(score.reshape(BLOCK // ROWS, ROWS, 2 * ROWS), limit[None])
                scores.append(score.reshape(BLOCK, 2 * ROWS))
            top = functools.reduce(
                jnp.maximum, [jnp.max(score, axis=-1, keepdims=True) for score in scores]
            )
            if not start:
                old = peak[rows, :]
                top = jnp.maximum(old, top)
            weights = [jnp.exp(score - top) for score in scores]
            added = sum(jnp.sum(weight, axis=-1, keepdims=True) for weight in weights)
            update = sum(
                jnp.dot(weight.astype(jnp.bfloat16), key, preferred_element_type=jnp.float32)
                for weight, key in zip(weights, keys)
            )
            if start:
                total[rows, :] = added
                acc[rows, :] = update
            else:
                rescale = jnp.exp(old - top)
                total[rows, :] = total[rows, :] * rescale + added
                acc[rows, :] = acc[rows, :] * rescale + update
            peak[rows, :] = top

    attend([z], True)

    @pl.loop(0, 6)
    def _(step):
        for half in range(2):
            for way in range(2):
                ring_arrival(way, step, half).wait_recv()
                ring_send(way, step + 1, half).start()
        attend([(z + 2 * NZ - 1 - step) % NZ, (z + 1 + step) % NZ], False)

    for half in range(2):
        for way in range(2):
            ring_arrival(way, 6, half).wait_recv()
    for way in range(2):
        ring_send(way, 7, way).start()
    attend([(z + NZ - 7) % NZ, (z + 7) % NZ], False)
    for way in range(2):
        ring_arrival(way, 7, way).wait_recv()
    attend([(z + 8) % NZ], False)

    for h in range(HEADS):
        rows = slice(h * ROWS, (h + 1) * ROWS)
        mixed = (acc[rows, :] / total[rows, :]).astype(jnp.bfloat16)
        out_ref[:, h * HDIM : (h + 1) * HDIM] = jnp.dot(
            mixed, expand_block(2 * h + 1), preferred_element_type=jnp.float32
        ).astype(jnp.bfloat16)

    for k in (1, 2, 3):
        quad_copy(k).wait_send()
        y_copy(ylo, yhi, k, y_peer(k)).wait_send()
        x_copy(x, k, x_peer(k)).wait_send()

    @pl.loop(1, NZ)
    def _(dz):
        remote(mine, mine, z_send.at[dz], z_recv.at[dz], right).wait_send()
        keys = kpos.at[z, yhi]
        remote(keys, keys, kz_send.at[dz], kz_recv.at[dz], right).wait_send()

    key_copy.wait_send()
    c_copy(core).wait_send()
    half_copy(yhi).wait_send()

    @pl.loop(0, 7)
    def _(step):
        for half in range(2):
            for way in range(2):
                ring_send(way, step, half).wait_send()

    for way in range(2):
        ring_send(way, 7, way).wait_send()


def body(arrivals, slots, lengths, w_joined, w_expand):
    vmem = pl.BlockSpec(memory_space=pltpu.VMEM)
    smem = pl.BlockSpec(memory_space=pltpu.SMEM)
    dma = pltpu.SemaphoreType.DMA
    return pl.pallas_call(
        kernel,
        out_shape=jax.ShapeDtypeStruct((ROWS, QCOLS), jnp.bfloat16),
        in_specs=[vmem, vmem, vmem, smem, vmem, vmem],
        out_specs=vmem,
        scratch_shapes=[
            pltpu.VMEM((4, 16, JPART), jnp.bfloat16),
            pltpu.VMEM((4, 16, JPART), jnp.bfloat16),
            pltpu.VMEM((2, 2, NZ, 2, 2, 2, 16, JPART + HDIM), jnp.bfloat16),
            pltpu.VMEM((ROWS, QCOLS + RANK), jnp.float32),
            pltpu.VMEM((NZ, 2, ROWS, RANK), jnp.bfloat16),
            pltpu.VMEM((NZ, 2, 8, ROWS), jnp.int32),
            pltpu.VMEM((HEADS * ROWS, RANK), jnp.bfloat16),
            pltpu.VMEM((HEADS * ROWS, 1), jnp.float32),
            pltpu.VMEM((HEADS * ROWS, 1), jnp.float32),
            pltpu.VMEM((HEADS * ROWS, RANK), jnp.float32),
            dma((4,)),
            dma((4,)),
            dma((NZ,)),
            dma((NZ,)),
            dma((NZ,)),
            dma((NZ,)),
            dma((4,)),
            dma((4,)),
            dma,
            dma,
            dma((4,)),
            dma((4,)),
            dma,
            dma,
            dma,
            dma,
            dma((2, 8, 2)),
            dma((2, 8, 2)),
        ],
        compiler_params=pltpu.CompilerParams(
            collective_id=0, has_side_effects=True, vmem_limit_bytes=48 * 1024 * 1024
        ),
    )(
        arrivals,
        slots.reshape(1, ROWS),
        slots.reshape(ROWS, 1),
        lengths,
        w_joined,
        w_expand,
    )


def solution(mesh):
    in_specs = (
        P(("group", "mp"), None),
        P(("group", "mp")),
        P("group", None),
        P("mp", "group"),
        P("mp", "group"),
    )
    out_specs = P(("group", "mp"), None)
    return jax.shard_map(body, mesh=mesh, in_specs=in_specs, out_specs=out_specs, check_vma=False)
```

```python
import functools

import jax
import jax.numpy as jnp
from jax import lax
from jax.experimental import pallas as pl
from jax.experimental.pallas import tpu as pltpu
from jax.sharding import PartitionSpec as P

HEADS = 8
HDIM = 128
QCOLS = HEADS * HDIM
RANK = 512
WIDTH = 2048
ROWS = 128
NZ = 16
NG = 16
SHARD = 96
QPART = 256
LPART = 128
KINDS = 3
ACROSS = ()
EPS = 1e-06
NEGATIVE = -1e30
OPEN = 3e38
MESH = pl.DeviceIdType.MESH
LAST = (((1,), (1,)), ((), ()))


def kernel(
    arrivals_ref,
    slot_row_ref,
    lengths_ref,
    joined_ref,
    expand_ref,
    out_ref,
    wide,
    shards,
    full_lat,
    full_map,
    full_query,
    query,
    lat,
    kpos,
    key_map,
    value_map,
    keys,
    values,
    peak,
    total,
    acc,
    g_send,
    g_recv,
    z_send,
    z_recv,
    kz_send,
    kz_recv,
    y_send,
    y_recv,
    ky_send,
    ky_recv,
    x_send,
    x_recv,
    c_send,
    c_recv,
    h_send,
    h_recv,
    r_send,
    r_recv,
    a_send,
    a_recv,
):
    g = lax.axis_index("group")
    m = lax.axis_index("mp")
    core, x, ylo = g % 2, (g // 2) % 4, g // 8
    z, yhi = m // 2, m % 2
    xl, xh = x % 2, x // 2
    y = yhi * 2 + ylo

    def group_of(ylo_, x_, core_):
        return (ylo_ * 4 + x_) * 2 + core_

    def mp_of(z_, yhi_):
        return z_ * 2 + yhi_

    def flip(value, bits, span):
        if span == 2:
            return (value + bits) % 2
        if bits == 2:
            return (value + 2) % 4
        low = value % 2
        if bits == 1:
            return value + 1 - 2 * low
        return 3 - value

    def y_peer(k):
        other = flip(y, k, 4)
        return (group_of(other % 2, x, core), mp_of(z, other // 2))

    def x_peer(k):
        return (group_of(ylo, flip(x, k, 4), core), m)

    core_peer = (group_of(ylo, x, 1 - core), m)
    half_peer = (g, mp_of(z, 1 - yhi))
    right = (g, mp_of((z + 1) % NZ, yhi))
    left = (g, mp_of((z + NZ - 1) % NZ, yhi))

    barrier = pltpu.get_barrier_semaphore()

    def greet(peer):
        pl.semaphore_signal(barrier, inc=1, device_id=peer, device_id_type=MESH)

    @pl.loop(1, NZ)
    def _(dz):
        greet((g, mp_of((z + dz) % NZ, yhi)))

    @pl.loop(1, NG)
    def _(k):
        greet(((g + k) % NG, m))

    greet(y_peer(2))
    greet(y_peer(3))

    def remote(src, dst, send, recv, peer):
        return pltpu.make_async_remote_copy(
            src_ref=src,
            dst_ref=dst,
            send_sem=send,
            recv_sem=recv,
            device_id=peer,
            device_id_type=MESH,
        )

    wide[...] = jnp.zeros_like(wide)
    wide[:, :, :SHARD] = joined_ref[...].astype(jnp.bfloat16).reshape(4, 16, SHARD)
    kpos[z, yhi] = jnp.broadcast_to(slot_row_ref[...], (8, ROWS))
    rows_at = g % 4
    part = g // 4
    shards[g] = wide[rows_at]

    def placing(first, count, start, width):
        row = lax.broadcasted_iota(jnp.int32, (count * HDIM, width), 0)
        col = lax.broadcasted_iota(jnp.int32, (count * HDIM, width), 1)
        inside = row % HDIM
        same = (inside < SHARD) & ((first + row // HDIM) * SHARD + inside == start + col)
        return jnp.where(same, 1.0, 0.0).astype(jnp.bfloat16)

    def placed(first, count, start, width):
        pieces = jnp.concatenate([shards[first + t] for t in range(count)], axis=1)
        return jnp.dot(
            pieces, placing(first, count, start, width), preferred_element_type=jnp.float32
        ).astype(jnp.bfloat16)

    pl.semaphore_wait(barrier, 32)

    @pl.loop(1, NG)
    def _(k):
        other = (g + k) % NG
        remote(
            wide.at[other % 4], shards.at[g], g_send.at[k], g_recv.at[k], (other, m)
        ).start()

    @pl.loop(1, NZ)
    def _(dz):
        peer = (g, mp_of((z + dz) % NZ, yhi))
        remote(kpos.at[z, yhi], kpos.at[z, yhi], kz_send.at[dz], kz_recv.at[dz], peer).start()

    @pl.loop(1, NG)
    def _(k):
        slot = shards.at[(g + NG - k) % NG]
        remote(slot, slot, g_send.at[k], g_recv.at[k], core_peer).wait_recv()

    fulls = (full_lat, full_map, full_query)

    def z_start(kind):
        @pl.loop(1, NZ)
        def _(dz):
            peer = (g, mp_of((z + dz) % NZ, yhi))
            mine = fulls[kind].at[ylo, xh, z, yhi, xl, core]
            remote(mine, mine, z_send.at[kind, dz], z_recv.at[kind, dz], peer).start()

    def z_wait(kind):
        @pl.loop(1, NZ)
        def _(dz):
            slot = fulls[kind].at[ylo, xh, (z + NZ - dz) % NZ, yhi, xl, core]
            remote(slot, slot, z_send.at[kind, dz], z_recv.at[kind, dz], right).wait_recv()

    lat_start = QCOLS + LPART * part
    full_lat[ylo, xh, z, yhi, xl, core] = placed(lat_start // SHARD, 2, lat_start, LPART)
    z_start(0)
    full_map[ylo, xh, z, yhi, xl, core] = expand_ref[...].astype(jnp.bfloat16)
    z_start(1)
    query_start = QPART * part
    full_query[ylo, xh, z, yhi, xl, core] = placed(query_start // SHARD, 4, query_start, QPART)
    z_start(2)

    def zs(half):
        return pl.ds(half * (NZ // 2), NZ // 2)

    def y_part(kind, half, y_, core_):
        if half == 0:
            return fulls[kind].at[y_ % 2, xh, zs(half), y_ // 2, xl, core_]
        return fulls[kind].at[y_ % 2, :, zs(half), y_ // 2, :, core_]

    def x_part(kind, half, x_, core_):
        if half == 0:
            return fulls[kind].at[:, x_ // 2, zs(half), :, x_ % 2, core_]
        return fulls[kind].at[ylo, x_ // 2, zs(half), yhi, x_ % 2, core_]

    def along(axis, kind, half, k):
        if axis == "y":
            block, peer, send, recv = y_part(kind, half, y, core), y_peer(k), y_send, y_recv
        else:
            block, peer, send, recv = x_part(kind, half, x, core), x_peer(k), x_send, x_recv
        return remote(block, block, send.at[kind, half, k], recv.at[kind, half, k], peer)

    def arrival(axis, kind, half, k):
        if axis == "y":
            block, send, recv = y_part(kind, half, flip(y, k, 4), core), y_send, y_recv
        else:
            block, send, recv = x_part(kind, half, flip(x, k, 4), core), x_send, x_recv
        return remote(block, block, send.at[kind, half, k], recv.at[kind, half, k], core_peer)

    order = (("y", "x"), ("x", "y"))

    def stage_start(kind, stage):
        for k in (1, 3, 2):
            for half in range(2):
                along(order[half][stage], kind, half, k).start()

    def stage_wait(kind, stage, half):
        for k in (1, 3, 2):
            arrival(order[half][stage], kind, half, k).wait_recv()

    def c_copy(kind, half, k, core_):
        if half == 0:
            block = x_part(kind, 0, flip(x, k, 4) if k else x, core_)
        else:
            block = y_part(kind, 1, flip(y, k, 4) if k else y, core_)
        return remote(
            block, block, c_send.at[kind, half, k], c_recv.at[kind, half, k], core_peer
        )

    def first_stage_end(kind):
        for half in range(2):
            stage_wait(kind, 0, half)
        stage_start(kind, 1)
        for half in range(2):
            c_copy(kind, half, 0, core).start()

    def second_stage_end(kind):
        for k in (1, 3, 2):
            for half in range(2):
                arrival(order[half][1], kind, half, k).wait_recv()
                c_copy(kind, half, k, core).start()

    def core_end(kind):
        for k in (0, 1, 3, 2):
            for half in range(2):
                c_copy(kind, half, k, 1 - core).wait_recv()

    rows_in = arrivals_ref[...].astype(jnp.float32)
    mean_sq = jnp.mean(rows_in * rows_in, axis=-1, keepdims=True)
    normed = (rows_in * lax.rsqrt(mean_sq + EPS)).astype(jnp.bfloat16)

    z_wait(0)
    stage_start(0, 0)
    first_stage_end(0)
    z_wait(1)
    stage_start(1, 0)
    z_wait(2)
    stage_start(2, 0)

    @pl.loop(1, NZ)
    def _(dz):
        block = kpos.at[(z + NZ - dz) % NZ, yhi]
        remote(block, block, kz_send.at[dz], kz_recv.at[dz], right).wait_recv()

    key_copy = remote(kpos.at[:, yhi], kpos.at[:, yhi], ky_send, ky_recv, half_peer)
    key_copy.start()
    second_stage_end(0)
    first_stage_end(1)
    core_end(0)

    raws = []
    for c in range(2):
        weight = jnp.concatenate(
            [full_lat[c, t].reshape(WIDTH, LPART) for t in range(2)], axis=1
        )
        raws.append(jnp.dot(normed, weight, preferred_element_type=jnp.float32))
    raw = jnp.concatenate(raws, axis=1)
    raw_sq = jnp.mean(raw * raw, axis=-1, keepdims=True)
    lat[z, yhi] = (raw * lax.rsqrt(raw_sq + EPS)).astype(jnp.bfloat16)

    def half_copy(yhi_):
        return remote(lat.at[z, yhi_], lat.at[z, yhi_], h_send, h_recv, half_peer)

    def ring_send(way, step, half):
        source = (z + NZ - step) % NZ if way == 0 else (z + step) % NZ
        block = lat.at[source, half]
        peer = right if way == 0 else left
        return remote(
            block, block, r_send.at[way, step, half], r_recv.at[way, step, half], peer
        )

    def ring_arrival(way, step, half):
        source = (z + 2 * NZ - 1 - step) % NZ if way == 0 else (z + 1 + step) % NZ
        block = lat.at[source, half]
        return remote(
            block, block, r_send.at[way, step, half], r_recv.at[way, step, half], right
        )

    def across(way, step, half):
        source = (z + 2 * NZ - 1 - step) % NZ if way == 0 else (z + 1 + step) % NZ
        block = lat.at[source, half]
        return remote(block, block, a_send.at[way, step], a_recv.at[way, step], half_peer)

    half_copy(yhi).start()
    ring_send(0, 0, yhi).start()
    ring_send(1, 0, yhi).start()
    half_copy(1 - yhi).wait_recv()
    if 0 not in ACROSS:
        ring_send(0, 0, 1 - yhi).start()
        ring_send(1, 0, 1 - yhi).start()
    remote(kpos.at[:, 1 - yhi], kpos.at[:, 1 - yhi], ky_send, ky_recv, half_peer).wait_recv()

    def pass_on(step):
        for way in range(2):
            ring_arrival(way, step, yhi).wait_recv()
            if step < 6:
                ring_send(way, step + 1, yhi).start()
            if step in ACROSS:
                across(way, step, yhi).start()
        for way in range(2):
            if step in ACROSS:
                across(way, step, 1 - yhi).wait_recv()
            else:
                ring_arrival(way, step, 1 - yhi).wait_recv()
            if step < 6 and step + 1 not in ACROSS:
                ring_send(way, step + 1, 1 - yhi).start()
        if step == 6:
            for way in range(2):
                ring_send(way, 7, way).start()

    first_stage_end(2)
    pass_on(0)
    second_stage_end(1)
    core_end(1)

    def expand_block(index):
        ylo_, x_, core_ = index // 8, (index // 2) % 4, index % 2
        return full_map[ylo_, x_ // 2, :, :, x_ % 2, core_].reshape(RANK, HDIM)

    eye_row = lax.broadcasted_iota(jnp.int32, (ROWS, ROWS), 0)
    eye_col = lax.broadcasted_iota(jnp.int32, (ROWS, ROWS), 1)
    diagonal = eye_row == eye_col
    eye = jnp.where(diagonal, 1.0, 0.0).astype(jnp.bfloat16)
    for h in range(HEADS):
        cols = slice(h * HDIM, (h + 1) * HDIM)
        key_map[:, cols] = expand_block(2 * h)
        value_map[cols, :] = lax.dot_general(
            eye, expand_block(2 * h + 1), LAST, preferred_element_type=jnp.float32
        ).astype(jnp.bfloat16)

    query_pos = slot_row_ref[...].astype(jnp.float32)
    slot_row = slot_row_ref[...]
    first = jnp.zeros_like(slot_row)
    end = lengths_ref[0, 0]
    for p in range(1, 4):
        first = jnp.where(slot_row >= end, end, first)
        end = end + lengths_ref[0, p]
    first = first.astype(jnp.float32)

    def widen(source):
        block = lat[source].reshape(2 * ROWS, RANK)
        keys[source] = jnp.dot(
            block, key_map[...], preferred_element_type=jnp.float32
        ).astype(jnp.bfloat16)
        values[source] = lax.dot_general(
            value_map[...], block, LAST, preferred_element_type=jnp.float32
        ).astype(jnp.bfloat16)

    def limit_of(source):
        limits = []
        for half in range(2):
            row = kpos[source, half][0:1].astype(jnp.float32)
            col = jnp.sum(jnp.where(diagonal, row, 0.0), axis=1, keepdims=True)
            allowed = (col <= query_pos) & (col >= first)
            limits.append(jnp.where(allowed, OPEN, NEGATIVE))
        return jnp.concatenate(limits, axis=0)

    def attend(sources, start):
        limits = [limit_of(source) for source in sources]
        for h in range(HEADS):
            cols = slice(h * HDIM, (h + 1) * HDIM)
            scores = [
                jnp.minimum(
                    lax.dot_general(
                        keys[source, :, cols],
                        query[:, cols],
                        LAST,
                        preferred_element_type=jnp.float32,
                    ),
                    limit,
                )
                for source, limit in zip(sources, limits)
            ]
            top = functools.reduce(
                jnp.maximum, [jnp.max(score, axis=0, keepdims=True) for score in scores]
            )
            if not start:
                old = peak[h]
                top = jnp.maximum(old, top)
            weights = [jnp.exp(score - top) for score in scores]
            added = sum(jnp.sum(weight, axis=0, keepdims=True) for weight in weights)
            update = sum(
                jnp.dot(
                    values[source, cols, :],
                    weight.astype(jnp.bfloat16),
                    preferred_element_type=jnp.float32,
                )
                for source, weight in zip(sources, weights)
            )
            if start:
                total[h] = added
                acc[h] = update
            else:
                rescale = jnp.exp(old - top)
                total[h] = total[h] * rescale + added
                acc[h] = acc[h] * rescale + update
            peak[h] = top

    def pair(step):
        return [(z + 2 * NZ - 1 - step) % NZ, (z + 1 + step) % NZ]

    def widen_pair(step):
        for source in pair(step):
            widen(source)

    widen(z)
    pass_on(1)
    widen_pair(0)
    pass_on(2)
    widen_pair(1)
    second_stage_end(2)
    pass_on(3)
    core_end(2)

    def project(c):
        weight = full_query[c // 2, c % 2].reshape(WIDTH, QPART)
        query[:, c * QPART : (c + 1) * QPART] = (
            jnp.dot(normed, weight, preferred_element_type=jnp.float32) * HDIM ** (-0.5)
        ).astype(jnp.bfloat16)

    project(0)
    project(1)
    widen_pair(2)
    pass_on(4)
    project(2)
    project(3)
    widen_pair(3)
    attend([z], True)
    attend(pair(0), False)
    pass_on(5)
    widen_pair(4)

    @pl.loop(1, 3)
    def _(step):
        attend(pair(step), False)

    pass_on(6)

    @pl.loop(5, 7)
    def _(step):
        widen_pair(step)

    @pl.loop(3, 7)
    def _(step):
        attend(pair(step), False)

    for way in range(2):
        ring_arrival(way, 7, way).wait_recv()
    widen((z + 8) % NZ)
    attend([(z + 8) % NZ], False)

    for h in range(HEADS):
        mixed = (acc[h] / total[h]).astype(jnp.bfloat16)
        out_ref[:, h * HDIM : (h + 1) * HDIM] = lax.dot_general(
            eye, mixed, LAST, preferred_element_type=jnp.float32
        ).astype(jnp.bfloat16)

    @pl.loop(1, NG)
    def _(k):
        remote(
            wide.at[(g + k) % 4], shards.at[g], g_send.at[k], g_recv.at[k], core_peer
        ).wait_send()

    @pl.loop(1, NZ)
    def _(dz):
        for kind in range(KINDS):
            mine = fulls[kind].at[ylo, xh, z, yhi, xl, core]
            remote(mine, mine, z_send.at[kind, dz], z_recv.at[kind, dz], right).wait_send()
        block = kpos.at[z, yhi]
        remote(block, block, kz_send.at[dz], kz_recv.at[dz], right).wait_send()

    key_copy.wait_send()
    for kind in range(KINDS):
        for half in range(2):
            for axis in ("x", "y"):
                for k in (1, 2, 3):
                    along(axis, kind, half, k).wait_send()
            for k in range(4):
                c_copy(kind, half, k, core).wait_send()
    half_copy(yhi).wait_send()

    for step in range(7):
        for way in range(2):
            ring_send(way, step, yhi).wait_send()
            if step in ACROSS:
                across(way, step, yhi).wait_send()
            else:
                ring_send(way, step, 1 - yhi).wait_send()

    for way in range(2):
        ring_send(way, 7, way).wait_send()


def body(arrivals, slots, lengths, w_joined, w_expand):
    vmem = pl.BlockSpec(memory_space=pltpu.VMEM)
    smem = pl.BlockSpec(memory_space=pltpu.SMEM)
    dma = pltpu.SemaphoreType.DMA
    return pl.pallas_call(
        kernel,
        out_shape=jax.ShapeDtypeStruct((ROWS, QCOLS), jnp.bfloat16),
        in_specs=[vmem, vmem, smem, vmem, vmem],
        out_specs=vmem,
        scratch_shapes=[
            pltpu.VMEM((4, 16, HDIM), jnp.bfloat16),
            pltpu.VMEM((NG, 16, HDIM), jnp.bfloat16),
            pltpu.VMEM((2, 2, NZ, 2, 2, 2, 16, LPART), jnp.bfloat16),
            pltpu.VMEM((2, 2, NZ, 2, 2, 2, 16, HDIM), jnp.bfloat16),
            pltpu.VMEM((2, 2, NZ, 2, 2, 2, 16, QPART), jnp.bfloat16),
            pltpu.VMEM((ROWS, QCOLS), jnp.bfloat16),
            pltpu.VMEM((NZ, 2, ROWS, RANK), jnp.bfloat16),
            pltpu.VMEM((NZ, 2, 8, ROWS), jnp.int32),
            pltpu.VMEM((RANK, QCOLS), jnp.bfloat16),
            pltpu.VMEM((QCOLS, RANK), jnp.bfloat16),
            pltpu.VMEM((NZ, 2 * ROWS, QCOLS), jnp.bfloat16),
            pltpu.VMEM((NZ, QCOLS, 2 * ROWS), jnp.bfloat16),
            pltpu.VMEM((HEADS, 1, ROWS), jnp.float32),
            pltpu.VMEM((HEADS, 1, ROWS), jnp.float32),
            pltpu.VMEM((HEADS, HDIM, ROWS), jnp.float32),
            dma((NG,)),
            dma((NG,)),
            dma((KINDS, NZ)),
            dma((KINDS, NZ)),
            dma((NZ,)),
            dma((NZ,)),
            dma((KINDS, 2, 4)),
            dma((KINDS, 2, 4)),
            dma,
            dma,
            dma((KINDS, 2, 4)),
            dma((KINDS, 2, 4)),
            dma((KINDS, 2, 4)),
            dma((KINDS, 2, 4)),
            dma,
            dma,
            dma((2, 8, 2)),
            dma((2, 8, 2)),
            dma((2, 8)),
            dma((2, 8)),
        ],
        compiler_params=pltpu.CompilerParams(
            collective_id=0, has_side_effects=True, vmem_limit_bytes=48 * 1024 * 1024
        ),
    )(
        arrivals,
        slots.reshape(1, ROWS),
        lengths,
        w_joined,
        w_expand,
    )


def solution(mesh):
    in_specs = (
        P(("group", "mp"), None),
        P(("group", "mp")),
        P("group", None),
        P("mp", "group"),
        P("mp", "group"),
    )
    out_specs = P(("group", "mp"), None)
    return jax.shard_map(body, mesh=mesh, in_specs=in_specs, out_specs=out_specs, check_vma=False)
```

```python
import functools

import jax
import jax.numpy as jnp
from jax import lax
from jax.experimental import pallas as pl
from jax.experimental.pallas import tpu as pltpu
from jax.sharding import PartitionSpec as P

HEADS = 8
HDIM = 128
QCOLS = HEADS * HDIM
RANK = 512
WIDTH = 2048
ROWS = 128
NZ = 16
NG = 16
SHARD = 96
QPART = 256
LPART = 128
KINDS = 3
TOGETHER = 8
EPS = 1e-06
NEGATIVE = -1e30
OPEN = 3e38
MESH = pl.DeviceIdType.MESH
LAST = (((1,), (1,)), ((), ()))


def kernel(
    arrivals_ref,
    slot_row_ref,
    lengths_ref,
    joined_ref,
    expand_ref,
    out_ref,
    wide,
    shards,
    full_lat,
    full_map,
    full_query,
    query,
    lat,
    kpos,
    key_map,
    value_map,
    keys,
    values,
    peak,
    total,
    acc,
    g_send,
    g_recv,
    z_send,
    z_recv,
    kz_send,
    kz_recv,
    y_send,
    y_recv,
    ky_send,
    ky_recv,
    x_send,
    x_recv,
    c_send,
    c_recv,
    h_send,
    h_recv,
    r_send,
    r_recv,
):
    g = lax.axis_index("group")
    m = lax.axis_index("mp")
    core, x, ylo = g % 2, (g // 2) % 4, g // 8
    z, yhi = m // 2, m % 2
    xl, xh = x % 2, x // 2
    y = yhi * 2 + ylo

    def group_of(ylo_, x_, core_):
        return (ylo_ * 4 + x_) * 2 + core_

    def mp_of(z_, yhi_):
        return z_ * 2 + yhi_

    def flip(value, bits, span):
        if span == 2:
            return (value + bits) % 2
        if bits == 2:
            return (value + 2) % 4
        low = value % 2
        if bits == 1:
            return value + 1 - 2 * low
        return 3 - value

    def y_peer(k):
        other = flip(y, k, 4)
        return (group_of(other % 2, x, core), mp_of(z, other // 2))

    def x_peer(k):
        return (group_of(ylo, flip(x, k, 4), core), m)

    core_peer = (group_of(ylo, x, 1 - core), m)
    half_peer = (g, mp_of(z, 1 - yhi))
    right = (g, mp_of((z + 1) % NZ, yhi))
    left = (g, mp_of((z + NZ - 1) % NZ, yhi))

    barrier = pltpu.get_barrier_semaphore()

    def greet(peer):
        pl.semaphore_signal(barrier, inc=1, device_id=peer, device_id_type=MESH)

    @pl.loop(1, NZ)
    def _(dz):
        greet((g, mp_of((z + dz) % NZ, yhi)))

    @pl.loop(1, NG)
    def _(k):
        greet(((g + k) % NG, m))

    greet(y_peer(2))
    greet(y_peer(3))

    def remote(src, dst, send, recv, peer):
        return pltpu.make_async_remote_copy(
            src_ref=src,
            dst_ref=dst,
            send_sem=send,
            recv_sem=recv,
            device_id=peer,
            device_id_type=MESH,
        )

    wide[...] = jnp.zeros_like(wide)
    wide[:, :, :SHARD] = joined_ref[...].astype(jnp.bfloat16).reshape(4, 16, SHARD)
    kpos[z, yhi] = jnp.broadcast_to(slot_row_ref[...], (8, ROWS))
    rows_at = g % 4
    part = g // 4
    shards[g] = wide[rows_at]

    def placing(first, count, start, width):
        row = lax.broadcasted_iota(jnp.int32, (count * HDIM, width), 0)
        col = lax.broadcasted_iota(jnp.int32, (count * HDIM, width), 1)
        inside = row % HDIM
        same = (inside < SHARD) & ((first + row // HDIM) * SHARD + inside == start + col)
        return jnp.where(same, 1.0, 0.0).astype(jnp.bfloat16)

    def placed(first, count, start, width):
        pieces = jnp.concatenate([shards[first + t] for t in range(count)], axis=1)
        return jnp.dot(
            pieces, placing(first, count, start, width), preferred_element_type=jnp.float32
        ).astype(jnp.bfloat16)

    pl.semaphore_wait(barrier, 32)

    @pl.loop(1, NG)
    def _(k):
        other = (g + k) % NG
        remote(
            wide.at[other % 4], shards.at[g], g_send.at[k], g_recv.at[k], (other, m)
        ).start()

    @pl.loop(1, NZ)
    def _(dz):
        peer = (g, mp_of((z + dz) % NZ, yhi))
        remote(kpos.at[z, yhi], kpos.at[z, yhi], kz_send.at[dz], kz_recv.at[dz], peer).start()

    @pl.loop(1, NG)
    def _(k):
        slot = shards.at[(g + NG - k) % NG]
        remote(slot, slot, g_send.at[k], g_recv.at[k], core_peer).wait_recv()

    fulls = (full_lat, full_map, full_query)

    def z_start(kind):
        @pl.loop(1, NZ)
        def _(dz):
            peer = (g, mp_of((z + dz) % NZ, yhi))
            mine = fulls[kind].at[ylo, xh, z, yhi, xl, core]
            remote(mine, mine, z_send.at[kind, dz], z_recv.at[kind, dz], peer).start()

    def z_wait(kind):
        @pl.loop(1, NZ)
        def _(dz):
            slot = fulls[kind].at[ylo, xh, (z + NZ - dz) % NZ, yhi, xl, core]
            remote(slot, slot, z_send.at[kind, dz], z_recv.at[kind, dz], right).wait_recv()

    lat_start = QCOLS + LPART * part
    full_lat[ylo, xh, z, yhi, xl, core] = placed(lat_start // SHARD, 2, lat_start, LPART)
    z_start(0)
    full_map[ylo, xh, z, yhi, xl, core] = expand_ref[...].astype(jnp.bfloat16)
    query_start = QPART * part
    full_query[ylo, xh, z, yhi, xl, core] = placed(query_start // SHARD, 4, query_start, QPART)

    def zs(half):
        return pl.ds(half * (NZ // 2), NZ // 2)

    def y_part(kind, half, y_, core_):
        if half == 0:
            return fulls[kind].at[y_ % 2, xh, zs(half), y_ // 2, xl, core_]
        return fulls[kind].at[y_ % 2, :, zs(half), y_ // 2, :, core_]

    def x_part(kind, half, x_, core_):
        if half == 0:
            return fulls[kind].at[:, x_ // 2, zs(half), :, x_ % 2, core_]
        return fulls[kind].at[ylo, x_ // 2, zs(half), yhi, x_ % 2, core_]

    def along(axis, kind, half, k):
        if axis == "y":
            block, peer, send, recv = y_part(kind, half, y, core), y_peer(k), y_send, y_recv
        else:
            block, peer, send, recv = x_part(kind, half, x, core), x_peer(k), x_send, x_recv
        return remote(block, block, send.at[kind, half, k], recv.at[kind, half, k], peer)

    def arrival(axis, kind, half, k):
        if axis == "y":
            block, send, recv = y_part(kind, half, flip(y, k, 4), core), y_send, y_recv
        else:
            block, send, recv = x_part(kind, half, flip(x, k, 4), core), x_send, x_recv
        return remote(block, block, send.at[kind, half, k], recv.at[kind, half, k], core_peer)

    order = (("y", "x"), ("x", "y"))

    def stage_start(kind, stage):
        for k in (1, 3, 2):
            for half in range(2):
                along(order[half][stage], kind, half, k).start()

    def stage_wait(kind, stage, half):
        for k in (1, 3, 2):
            arrival(order[half][stage], kind, half, k).wait_recv()

    def c_copy(kind, half, k, core_):
        if half == 0:
            block = x_part(kind, 0, flip(x, k, 4) if k else x, core_)
        else:
            block = y_part(kind, 1, flip(y, k, 4) if k else y, core_)
        return remote(
            block, block, c_send.at[kind, half, k], c_recv.at[kind, half, k], core_peer
        )

    def first_stage_end(kind):
        for half in range(2):
            stage_wait(kind, 0, half)
        stage_start(kind, 1)
        for half in range(2):
            c_copy(kind, half, 0, core).start()

    def second_stage_end(kind):
        for k in (1, 3, 2):
            for half in range(2):
                arrival(order[half][1], kind, half, k).wait_recv()
                c_copy(kind, half, k, core).start()

    def core_end(kind):
        for k in (0, 1, 3, 2):
            for half in range(2):
                c_copy(kind, half, k, 1 - core).wait_recv()

    rows_in = arrivals_ref[...].astype(jnp.float32)
    mean_sq = jnp.mean(rows_in * rows_in, axis=-1, keepdims=True)
    normed = (rows_in * lax.rsqrt(mean_sq + EPS)).astype(jnp.bfloat16)

    z_wait(0)
    stage_start(0, 0)
    z_start(1)
    z_start(2)
    first_stage_end(0)
    z_wait(1)
    stage_start(1, 0)

    @pl.loop(1, NZ)
    def _(dz):
        block = kpos.at[(z + NZ - dz) % NZ, yhi]
        remote(block, block, kz_send.at[dz], kz_recv.at[dz], right).wait_recv()

    key_copy = remote(kpos.at[:, yhi], kpos.at[:, yhi], ky_send, ky_recv, half_peer)
    key_copy.start()
    second_stage_end(0)
    core_end(0)

    raws = []
    for c in range(2):
        weight = jnp.concatenate(
            [full_lat[c, t].reshape(WIDTH, LPART) for t in range(2)], axis=1
        )
        raws.append(jnp.dot(normed, weight, preferred_element_type=jnp.float32))
    raw = jnp.concatenate(raws, axis=1)
    raw_sq = jnp.mean(raw * raw, axis=-1, keepdims=True)
    lat[z, yhi] = (raw * lax.rsqrt(raw_sq + EPS)).astype(jnp.bfloat16)

    def half_copy(yhi_):
        return remote(lat.at[z, yhi_], lat.at[z, yhi_], h_send, h_recv, half_peer)

    def ring_send(way, step, half):
        source = (z + NZ - step) % NZ if way == 0 else (z + step) % NZ
        block = lat.at[source, half]
        peer = right if way == 0 else left
        return remote(
            block, block, r_send.at[way, step, half], r_recv.at[way, step, half], peer
        )

    def ring_arrival(way, step, half):
        source = (z + 2 * NZ - 1 - step) % NZ if way == 0 else (z + 1 + step) % NZ
        block = lat.at[source, half]
        return remote(
            block, block, r_send.at[way, step, half], r_recv.at[way, step, half], right
        )

    half_copy(yhi).start()
    ring_send(0, 0, yhi).start()
    ring_send(1, 0, yhi).start()
    first_stage_end(1)
    z_wait(2)
    stage_start(2, 0)
    half_copy(1 - yhi).wait_recv()
    ring_send(0, 0, 1 - yhi).start()
    ring_send(1, 0, 1 - yhi).start()
    remote(kpos.at[:, 1 - yhi], kpos.at[:, 1 - yhi], ky_send, ky_recv, half_peer).wait_recv()

    def pass_on(step):
        for half in (yhi, 1 - yhi):
            for way in range(2):
                ring_arrival(way, step, half).wait_recv()
                if step < 6:
                    ring_send(way, step + 1, half).start()
        if step == 6:
            for way in range(2):
                ring_send(way, 7, way).start()

    pass_on(0)
    second_stage_end(1)
    first_stage_end(2)
    core_end(1)

    def expand_block(index):
        ylo_, x_, core_ = index // 8, (index // 2) % 4, index % 2
        return full_map[ylo_, x_ // 2, :, :, x_ % 2, core_].reshape(RANK, HDIM)

    eye_row = lax.broadcasted_iota(jnp.int32, (ROWS, ROWS), 0)
    eye_col = lax.broadcasted_iota(jnp.int32, (ROWS, ROWS), 1)
    diagonal = eye_row == eye_col
    eye = jnp.where(diagonal, 1.0, 0.0).astype(jnp.bfloat16)
    for h in range(HEADS):
        cols = slice(h * HDIM, (h + 1) * HDIM)
        key_map[:, cols] = expand_block(2 * h)
        value_map[cols, :] = lax.dot_general(
            eye, expand_block(2 * h + 1), LAST, preferred_element_type=jnp.float32
        ).astype(jnp.bfloat16)

    query_pos = slot_row_ref[...].astype(jnp.float32)
    slot_row = slot_row_ref[...]
    first = jnp.zeros_like(slot_row)
    end = lengths_ref[0, 0]
    for p in range(1, 4):
        first = jnp.where(slot_row >= end, end, first)
        end = end + lengths_ref[0, p]
    first = first.astype(jnp.float32)

    def widen(source):
        block = lat[source].reshape(2 * ROWS, RANK)
        keys[source] = jnp.dot(
            block, key_map[...], preferred_element_type=jnp.float32
        ).astype(jnp.bfloat16)
        values[source] = lax.dot_general(
            value_map[...], block, LAST, preferred_element_type=jnp.float32
        ).astype(jnp.bfloat16)

    def limit_of(source):
        limits = []
        for half in range(2):
            row = kpos[source, half][0:1].astype(jnp.float32)
            col = jnp.sum(jnp.where(diagonal, row, 0.0), axis=1, keepdims=True)
            allowed = (col <= query_pos) & (col >= first)
            limits.append(jnp.where(allowed, OPEN, NEGATIVE))
        return jnp.concatenate(limits, axis=0)

    def attend(sources, start):
        limits = [limit_of(source) for source in sources]
        def scores_of(h):
            cols = slice(h * HDIM, (h + 1) * HDIM)
            return [
                jnp.minimum(
                    lax.dot_general(
                        keys[source, :, cols],
                        query[:, cols],
                        LAST,
                        preferred_element_type=jnp.float32,
                    ),
                    limit,
                )
                for source, limit in zip(sources, limits)
            ]

        def weigh(h, scores):
            top = functools.reduce(
                jnp.maximum, [jnp.max(score, axis=0, keepdims=True) for score in scores]
            )
            if not start:
                old = peak[h]
                top = jnp.maximum(old, top)
            weights = [jnp.exp(score - top) for score in scores]
            added = sum(jnp.sum(weight, axis=0, keepdims=True) for weight in weights)
            rescale = None
            if start:
                total[h] = added
            else:
                rescale = jnp.exp(old - top)
                total[h] = total[h] * rescale + added
            peak[h] = top
            return [weight.astype(jnp.bfloat16) for weight in weights], rescale

        def gather(h, weights, rescale):
            cols = slice(h * HDIM, (h + 1) * HDIM)
            update = sum(
                jnp.dot(
                    values[source, cols, :], weight, preferred_element_type=jnp.float32
                )
                for source, weight in zip(sources, weights)
            )
            acc[h] = update if start else acc[h] * rescale + update

        for first_head in range(0, HEADS, TOGETHER):
            heads = range(first_head, first_head + TOGETHER)
            scored = [scores_of(h) for h in heads]
            weighed = [weigh(h, scores) for h, scores in zip(heads, scored)]
            for h, (weights, rescale) in zip(heads, weighed):
                gather(h, weights, rescale)

    def pair(step):
        return [(z + 2 * NZ - 1 - step) % NZ, (z + 1 + step) % NZ]

    def widen_pair(step):
        for source in pair(step):
            widen(source)

    pass_on(1)
    widen(z)
    widen_pair(0)
    pass_on(2)
    widen_pair(1)
    second_stage_end(2)
    pass_on(3)
    widen_pair(2)
    core_end(2)

    def project(c):
        weight = full_query[c // 2, c % 2].reshape(WIDTH, QPART)
        query[:, c * QPART : (c + 1) * QPART] = (
            jnp.dot(normed, weight, preferred_element_type=jnp.float32) * HDIM ** (-0.5)
        ).astype(jnp.bfloat16)

    for c in range(4):
        project(c)
    attend([z], True)
    pass_on(4)
    widen_pair(3)

    @pl.loop(0, 3)
    def _(step):
        attend(pair(step), False)

    pass_on(5)

    @pl.loop(4, 6)
    def _(step):
        widen_pair(step)
        attend(pair(step - 1), False)

    pass_on(6)
    widen_pair(6)

    @pl.loop(5, 7)
    def _(step):
        attend(pair(step), False)

    for way in range(2):
        ring_arrival(way, 7, way).wait_recv()
    widen((z + 8) % NZ)
    attend([(z + 8) % NZ], False)

    for h in range(HEADS):
        mixed = (acc[h] / total[h]).astype(jnp.bfloat16)
        out_ref[:, h * HDIM : (h + 1) * HDIM] = lax.dot_general(
            eye, mixed, LAST, preferred_element_type=jnp.float32
        ).astype(jnp.bfloat16)

    @pl.loop(1, NG)
    def _(k):
        remote(
            wide.at[(g + k) % 4], shards.at[g], g_send.at[k], g_recv.at[k], core_peer
        ).wait_send()

    @pl.loop(1, NZ)
    def _(dz):
        for kind in range(KINDS):
            mine = fulls[kind].at[ylo, xh, z, yhi, xl, core]
            remote(mine, mine, z_send.at[kind, dz], z_recv.at[kind, dz], right).wait_send()
        block = kpos.at[z, yhi]
        remote(block, block, kz_send.at[dz], kz_recv.at[dz], right).wait_send()

    key_copy.wait_send()
    for kind in range(KINDS):
        for half in range(2):
            for axis in ("x", "y"):
                for k in (1, 2, 3):
                    along(axis, kind, half, k).wait_send()
            for k in range(4):
                c_copy(kind, half, k, core).wait_send()
    half_copy(yhi).wait_send()

    @pl.loop(0, 7)
    def _(step):
        for half in range(2):
            for way in range(2):
                ring_send(way, step, half).wait_send()

    for way in range(2):
        ring_send(way, 7, way).wait_send()


def body(arrivals, slots, lengths, w_joined, w_expand):
    vmem = pl.BlockSpec(memory_space=pltpu.VMEM)
    smem = pl.BlockSpec(memory_space=pltpu.SMEM)
    dma = pltpu.SemaphoreType.DMA
    return pl.pallas_call(
        kernel,
        out_shape=jax.ShapeDtypeStruct((ROWS, QCOLS), jnp.bfloat16),
        in_specs=[vmem, vmem, smem, vmem, vmem],
        out_specs=vmem,
        scratch_shapes=[
            pltpu.VMEM((4, 16, HDIM), jnp.bfloat16),
            pltpu.VMEM((NG, 16, HDIM), jnp.bfloat16),
            pltpu.VMEM((2, 2, NZ, 2, 2, 2, 16, LPART), jnp.bfloat16),
            pltpu.VMEM((2, 2, NZ, 2, 2, 2, 16, HDIM), jnp.bfloat16),
            pltpu.VMEM((2, 2, NZ, 2, 2, 2, 16, QPART), jnp.bfloat16),
            pltpu.VMEM((ROWS, QCOLS), jnp.bfloat16),
            pltpu.VMEM((NZ, 2, ROWS, RANK), jnp.bfloat16),
            pltpu.VMEM((NZ, 2, 8, ROWS), jnp.int32),
            pltpu.VMEM((RANK, QCOLS), jnp.bfloat16),
            pltpu.VMEM((QCOLS, RANK), jnp.bfloat16),
            pltpu.VMEM((NZ, 2 * ROWS, QCOLS), jnp.bfloat16),
            pltpu.VMEM((NZ, QCOLS, 2 * ROWS), jnp.bfloat16),
            pltpu.VMEM((HEADS, 1, ROWS), jnp.float32),
            pltpu.VMEM((HEADS, 1, ROWS), jnp.float32),
            pltpu.VMEM((HEADS, HDIM, ROWS), jnp.float32),
            dma((NG,)),
            dma((NG,)),
            dma((KINDS, NZ)),
            dma((KINDS, NZ)),
            dma((NZ,)),
            dma((NZ,)),
            dma((KINDS, 2, 4)),
            dma((KINDS, 2, 4)),
            dma,
            dma,
            dma((KINDS, 2, 4)),
            dma((KINDS, 2, 4)),
            dma((KINDS, 2, 4)),
            dma((KINDS, 2, 4)),
            dma,
            dma,
            dma((2, 8, 2)),
            dma((2, 8, 2)),
        ],
        compiler_params=pltpu.CompilerParams(
            collective_id=0, has_side_effects=True, vmem_limit_bytes=48 * 1024 * 1024
        ),
    )(
        arrivals,
        slots.reshape(1, ROWS),
        lengths,
        w_joined,
        w_expand,
    )


def solution(mesh):
    in_specs = (
        P(("group", "mp"), None),
        P(("group", "mp")),
        P("group", None),
        P("mp", "group"),
        P("mp", "group"),
    )
    out_specs = P(("group", "mp"), None)
    return jax.shard_map(body, mesh=mesh, in_specs=in_specs, out_specs=out_specs, check_vma=False)
```

```python
import functools

import jax
import jax.numpy as jnp
from jax import lax
from jax.experimental import pallas as pl
from jax.experimental.pallas import tpu as pltpu
from jax.sharding import PartitionSpec as P

HEADS = 8
HDIM = 128
QCOLS = HEADS * HDIM
RANK = 512
WIDTH = 2048
ROWS = 128
NZ = 16
NG = 16
SHARD = 96
QPART = 256
LPART = 128
KINDS = 3
TOGETHER = 8
EPS = 1e-06
NEGATIVE = -1e30
OPEN = 3e38
MESH = pl.DeviceIdType.MESH
LAST = (((1,), (1,)), ((), ()))


def kernel(
    arrivals_ref,
    slot_row_ref,
    lengths_ref,
    joined_ref,
    expand_ref,
    out_ref,
    wide,
    shards,
    full_lat,
    full_map,
    full_query,
    query,
    lat,
    kpos,
    key_map,
    value_map,
    keys,
    values,
    peak,
    total,
    acc,
    g_send,
    g_recv,
    z_send,
    z_recv,
    kz_send,
    kz_recv,
    y_send,
    y_recv,
    ky_send,
    ky_recv,
    x_send,
    x_recv,
    c_send,
    c_recv,
    h_send,
    h_recv,
    r_send,
    r_recv,
):
    g = lax.axis_index("group")
    m = lax.axis_index("mp")
    core, x, ylo = g % 2, (g // 2) % 4, g // 8
    z, yhi = m // 2, m % 2
    xl, xh = x % 2, x // 2
    y = yhi * 2 + ylo

    def group_of(ylo_, x_, core_):
        return (ylo_ * 4 + x_) * 2 + core_

    def mp_of(z_, yhi_):
        return z_ * 2 + yhi_

    def flip(value, bits, span):
        if span == 2:
            return (value + bits) % 2
        if bits == 2:
            return (value + 2) % 4
        low = value % 2
        if bits == 1:
            return value + 1 - 2 * low
        return 3 - value

    def y_peer(k):
        other = flip(y, k, 4)
        return (group_of(other % 2, x, core), mp_of(z, other // 2))

    def x_peer(k):
        return (group_of(ylo, flip(x, k, 4), core), m)

    core_peer = (group_of(ylo, x, 1 - core), m)
    half_peer = (g, mp_of(z, 1 - yhi))
    right = (g, mp_of((z + 1) % NZ, yhi))
    left = (g, mp_of((z + NZ - 1) % NZ, yhi))

    barrier = pltpu.get_barrier_semaphore()

    def greet(peer):
        pl.semaphore_signal(barrier, inc=1, device_id=peer, device_id_type=MESH)

    @pl.loop(1, NZ)
    def _(dz):
        greet((g, mp_of((z + dz) % NZ, yhi)))

    @pl.loop(1, NG)
    def _(k):
        greet(((g + k) % NG, m))

    greet(y_peer(2))
    greet(y_peer(3))

    def remote(src, dst, send, recv, peer):
        return pltpu.make_async_remote_copy(
            src_ref=src,
            dst_ref=dst,
            send_sem=send,
            recv_sem=recv,
            device_id=peer,
            device_id_type=MESH,
        )

    wide[...] = jnp.zeros_like(wide)
    wide[:, :, :SHARD] = joined_ref[...].astype(jnp.bfloat16).reshape(4, 16, SHARD)
    kpos[z, yhi] = jnp.broadcast_to(slot_row_ref[...], (8, ROWS))
    rows_at = g % 4
    part = g // 4
    shards[g] = wide[rows_at]

    def placing(first, count, start, width):
        row = lax.broadcasted_iota(jnp.int32, (count * HDIM, width), 0)
        col = lax.broadcasted_iota(jnp.int32, (count * HDIM, width), 1)
        inside = row % HDIM
        same = (inside < SHARD) & ((first + row // HDIM) * SHARD + inside == start + col)
        return jnp.where(same, 1.0, 0.0).astype(jnp.bfloat16)

    def placed(first, count, start, width):
        pieces = jnp.concatenate([shards[first + t] for t in range(count)], axis=1)
        return jnp.dot(
            pieces, placing(first, count, start, width), preferred_element_type=jnp.float32
        ).astype(jnp.bfloat16)

    pl.semaphore_wait(barrier, 32)

    @pl.loop(1, NG)
    def _(k):
        other = (g + k) % NG
        remote(
            wide.at[other % 4], shards.at[g], g_send.at[k], g_recv.at[k], (other, m)
        ).start()

    @pl.loop(1, NZ)
    def _(dz):
        peer = (g, mp_of((z + dz) % NZ, yhi))
        remote(kpos.at[z, yhi], kpos.at[z, yhi], kz_send.at[dz], kz_recv.at[dz], peer).start()

    @pl.loop(1, NG)
    def _(k):
        slot = shards.at[(g + NG - k) % NG]
        remote(slot, slot, g_send.at[k], g_recv.at[k], core_peer).wait_recv()

    fulls = (full_lat, full_map, full_query)

    def z_start(kind):
        @pl.loop(1, NZ)
        def _(dz):
            peer = (g, mp_of((z + dz) % NZ, yhi))
            mine = fulls[kind].at[ylo, xh, z, yhi, xl, core]
            remote(mine, mine, z_send.at[kind, dz], z_recv.at[kind, dz], peer).start()

    def z_wait(kind):
        @pl.loop(1, NZ)
        def _(dz):
            slot = fulls[kind].at[ylo, xh, (z + NZ - dz) % NZ, yhi, xl, core]
            remote(slot, slot, z_send.at[kind, dz], z_recv.at[kind, dz], right).wait_recv()

    lat_start = QCOLS + LPART * part
    full_lat[ylo, xh, z, yhi, xl, core] = placed(lat_start // SHARD, 2, lat_start, LPART)
    z_start(0)
    full_map[ylo, xh, z, yhi, xl, core] = expand_ref[...].astype(jnp.bfloat16)
    query_start = QPART * part
    full_query[ylo, xh, z, yhi, xl, core] = placed(query_start // SHARD, 4, query_start, QPART)

    def zs(half):
        return pl.ds(half * (NZ // 2), NZ // 2)

    def y_part(kind, half, y_, core_):
        if half == 0:
            return fulls[kind].at[y_ % 2, xh, zs(half), y_ // 2, xl, core_]
        return fulls[kind].at[y_ % 2, :, zs(half), y_ // 2, :, core_]

    def x_part(kind, half, x_, core_):
        if half == 0:
            return fulls[kind].at[:, x_ // 2, zs(half), :, x_ % 2, core_]
        return fulls[kind].at[ylo, x_ // 2, zs(half), yhi, x_ % 2, core_]

    def along(axis, kind, half, k):
        if axis == "y":
            block, peer, send, recv = y_part(kind, half, y, core), y_peer(k), y_send, y_recv
        else:
            block, peer, send, recv = x_part(kind, half, x, core), x_peer(k), x_send, x_recv
        return remote(block, block, send.at[kind, half, k], recv.at[kind, half, k], peer)

    def arrival(axis, kind, half, k):
        if axis == "y":
            block, send, recv = y_part(kind, half, flip(y, k, 4), core), y_send, y_recv
        else:
            block, send, recv = x_part(kind, half, flip(x, k, 4), core), x_send, x_recv
        return remote(block, block, send.at[kind, half, k], recv.at[kind, half, k], core_peer)

    order = (("y", "x"), ("x", "y"))

    def stage_start(kind, stage):
        for k in (2, 1, 3):
            for half in range(2):
                along(order[half][stage], kind, half, k).start()

    def stage_wait(kind, stage, half):
        for k in (1, 3, 2):
            arrival(order[half][stage], kind, half, k).wait_recv()

    def c_copy(kind, half, k, core_):
        if half == 0:
            block = x_part(kind, 0, flip(x, k, 4) if k else x, core_)
        else:
            block = y_part(kind, 1, flip(y, k, 4) if k else y, core_)
        return remote(
            block, block, c_send.at[kind, half, k], c_recv.at[kind, half, k], core_peer
        )

    def first_stage_end(kind):
        for half in range(2):
            stage_wait(kind, 0, half)
        stage_start(kind, 1)
        for half in range(2):
            c_copy(kind, half, 0, core).start()

    def second_stage_end(kind):
        for k in (1, 3, 2):
            for half in range(2):
                arrival(order[half][1], kind, half, k).wait_recv()
                c_copy(kind, half, k, core).start()

    def core_end(kind):
        for k in (0, 1, 3, 2):
            for half in range(2):
                c_copy(kind, half, k, 1 - core).wait_recv()

    rows_in = arrivals_ref[...].astype(jnp.float32)
    mean_sq = jnp.mean(rows_in * rows_in, axis=-1, keepdims=True)
    normed = (rows_in * lax.rsqrt(mean_sq + EPS)).astype(jnp.bfloat16)

    z_wait(0)
    stage_start(0, 0)
    z_start(1)
    z_start(2)
    first_stage_end(0)
    z_wait(1)
    stage_start(1, 0)

    @pl.loop(1, NZ)
    def _(dz):
        block = kpos.at[(z + NZ - dz) % NZ, yhi]
        remote(block, block, kz_send.at[dz], kz_recv.at[dz], right).wait_recv()

    key_copy = remote(kpos.at[:, yhi], kpos.at[:, yhi], ky_send, ky_recv, half_peer)
    key_copy.start()
    second_stage_end(0)
    core_end(0)

    raws = []
    for c in range(2):
        weight = jnp.concatenate(
            [full_lat[c, t].reshape(WIDTH, LPART) for t in range(2)], axis=1
        )
        raws.append(jnp.dot(normed, weight, preferred_element_type=jnp.float32))
    raw = jnp.concatenate(raws, axis=1)
    raw_sq = jnp.mean(raw * raw, axis=-1, keepdims=True)
    lat[z, yhi] = (raw * lax.rsqrt(raw_sq + EPS)).astype(jnp.bfloat16)

    def half_copy(yhi_):
        return remote(lat.at[z, yhi_], lat.at[z, yhi_], h_send, h_recv, half_peer)

    def ring_send(way, step, half):
        source = (z + NZ - step) % NZ if way == 0 else (z + step) % NZ
        block = lat.at[source, half]
        peer = right if way == 0 else left
        return remote(
            block, block, r_send.at[way, step, half], r_recv.at[way, step, half], peer
        )

    def ring_arrival(way, step, half):
        source = (z + 2 * NZ - 1 - step) % NZ if way == 0 else (z + 1 + step) % NZ
        block = lat.at[source, half]
        return remote(
            block, block, r_send.at[way, step, half], r_recv.at[way, step, half], right
        )

    half_copy(yhi).start()
    ring_send(0, 0, yhi).start()
    ring_send(1, 0, yhi).start()
    first_stage_end(1)
    z_wait(2)
    stage_start(2, 0)
    half_copy(1 - yhi).wait_recv()
    ring_send(0, 0, 1 - yhi).start()
    ring_send(1, 0, 1 - yhi).start()
    remote(kpos.at[:, 1 - yhi], kpos.at[:, 1 - yhi], ky_send, ky_recv, half_peer).wait_recv()

    def pass_on(step):
        for half in (yhi, 1 - yhi):
            for way in range(2):
                ring_arrival(way, step, half).wait_recv()
                if step < 6:
                    ring_send(way, step + 1, half).start()
        if step == 6:
            for way in range(2):
                ring_send(way, 7, way).start()

    pass_on(0)
    second_stage_end(1)
    first_stage_end(2)
    core_end(1)

    def expand_block(index):
        ylo_, x_, core_ = index // 8, (index // 2) % 4, index % 2
        return full_map[ylo_, x_ // 2, :, :, x_ % 2, core_].reshape(RANK, HDIM)

    eye_row = lax.broadcasted_iota(jnp.int32, (ROWS, ROWS), 0)
    eye_col = lax.broadcasted_iota(jnp.int32, (ROWS, ROWS), 1)
    diagonal = eye_row == eye_col
    eye = jnp.where(diagonal, 1.0, 0.0).astype(jnp.bfloat16)
    for h in range(HEADS):
        cols = slice(h * HDIM, (h + 1) * HDIM)
        key_map[:, cols] = expand_block(2 * h)
        value_map[cols, :] = lax.dot_general(
            eye, expand_block(2 * h + 1), LAST, preferred_element_type=jnp.float32
        ).astype(jnp.bfloat16)

    query_pos = slot_row_ref[...].astype(jnp.float32)
    slot_row = slot_row_ref[...]
    first = jnp.zeros_like(slot_row)
    end = lengths_ref[0, 0]
    for p in range(1, 4):
        first = jnp.where(slot_row >= end, end, first)
        end = end + lengths_ref[0, p]
    first = first.astype(jnp.float32)

    def widen(source):
        block = lat[source].reshape(2 * ROWS, RANK)
        keys[source] = jnp.dot(
            block, key_map[...], preferred_element_type=jnp.float32
        ).astype(jnp.bfloat16)
        values[source] = lax.dot_general(
            value_map[...], block, LAST, preferred_element_type=jnp.float32
        ).astype(jnp.bfloat16)

    def limit_of(source):
        limits = []
        for half in range(2):
            row = kpos[source, half][0:1].astype(jnp.float32)
            col = jnp.sum(jnp.where(diagonal, row, 0.0), axis=1, keepdims=True)
            allowed = (col <= query_pos) & (col >= first)
            limits.append(jnp.where(allowed, OPEN, NEGATIVE))
        return jnp.concatenate(limits, axis=0)

    def attend(sources, start):
        limits = [limit_of(source) for source in sources]
        def scores_of(h):
            cols = slice(h * HDIM, (h + 1) * HDIM)
            return [
                jnp.minimum(
                    lax.dot_general(
                        keys[source, :, cols],
                        query[:, cols],
                        LAST,
                        preferred_element_type=jnp.float32,
                    ),
                    limit,
                )
                for source, limit in zip(sources, limits)
            ]

        def weigh(h, scores):
            top = functools.reduce(
                jnp.maximum, [jnp.max(score, axis=0, keepdims=True) for score in scores]
            )
            if not start:
                old = peak[h]
                top = jnp.maximum(old, top)
            weights = [jnp.exp(score - top) for score in scores]
            added = sum(jnp.sum(weight, axis=0, keepdims=True) for weight in weights)
            rescale = None
            if start:
                total[h] = added
            else:
                rescale = jnp.exp(old - top)
                total[h] = total[h] * rescale + added
            peak[h] = top
            return [weight.astype(jnp.bfloat16) for weight in weights], rescale

        def gather(h, weights, rescale):
            cols = slice(h * HDIM, (h + 1) * HDIM)
            update = sum(
                jnp.dot(
                    values[source, cols, :], weight, preferred_element_type=jnp.float32
                )
                for source, weight in zip(sources, weights)
            )
            acc[h] = update if start else acc[h] * rescale + update

        for first_head in range(0, HEADS, TOGETHER):
            heads = range(first_head, first_head + TOGETHER)
            scored = [scores_of(h) for h in heads]
            weighed = [weigh(h, scores) for h, scores in zip(heads, scored)]
            for h, (weights, rescale) in zip(heads, weighed):
                gather(h, weights, rescale)

    def pair(step):
        return [(z + 2 * NZ - 1 - step) % NZ, (z + 1 + step) % NZ]

    def widen_pair(step):
        for source in pair(step):
            widen(source)

    pass_on(1)
    widen(z)
    widen_pair(0)
    pass_on(2)
    widen_pair(1)
    second_stage_end(2)
    pass_on(3)
    widen_pair(2)
    core_end(2)

    def project(c):
        weight = full_query[c // 2, c % 2].reshape(WIDTH, QPART)
        query[:, c * QPART : (c + 1) * QPART] = (
            jnp.dot(normed, weight, preferred_element_type=jnp.float32) * HDIM ** (-0.5)
        ).astype(jnp.bfloat16)

    for c in range(4):
        project(c)
    attend([z], True)
    pass_on(4)
    widen_pair(3)

    @pl.loop(0, 3)
    def _(step):
        attend(pair(step), False)

    pass_on(5)

    @pl.loop(4, 6)
    def _(step):
        widen_pair(step)
        attend(pair(step - 1), False)

    pass_on(6)
    widen_pair(6)

    @pl.loop(5, 7)
    def _(step):
        attend(pair(step), False)

    for way in range(2):
        ring_arrival(way, 7, way).wait_recv()
    widen((z + 8) % NZ)
    attend([(z + 8) % NZ], False)

    for h in range(HEADS):
        mixed = (acc[h] / total[h]).astype(jnp.bfloat16)
        out_ref[:, h * HDIM : (h + 1) * HDIM] = lax.dot_general(
            eye, mixed, LAST, preferred_element_type=jnp.float32
        ).astype(jnp.bfloat16)

    @pl.loop(1, NG)
    def _(k):
        remote(
            wide.at[(g + k) % 4], shards.at[g], g_send.at[k], g_recv.at[k], core_peer
        ).wait_send()

    @pl.loop(1, NZ)
    def _(dz):
        for kind in range(KINDS):
            mine = fulls[kind].at[ylo, xh, z, yhi, xl, core]
            remote(mine, mine, z_send.at[kind, dz], z_recv.at[kind, dz], right).wait_send()
        block = kpos.at[z, yhi]
        remote(block, block, kz_send.at[dz], kz_recv.at[dz], right).wait_send()

    key_copy.wait_send()
    for kind in range(KINDS):
        for half in range(2):
            for axis in ("x", "y"):
                for k in (1, 2, 3):
                    along(axis, kind, half, k).wait_send()
            for k in range(4):
                c_copy(kind, half, k, core).wait_send()
    half_copy(yhi).wait_send()

    @pl.loop(0, 7)
    def _(step):
        for half in range(2):
            for way in range(2):
                ring_send(way, step, half).wait_send()

    for way in range(2):
        ring_send(way, 7, way).wait_send()


def body(arrivals, slots, lengths, w_joined, w_expand):
    vmem = pl.BlockSpec(memory_space=pltpu.VMEM)
    smem = pl.BlockSpec(memory_space=pltpu.SMEM)
    dma = pltpu.SemaphoreType.DMA
    return pl.pallas_call(
        kernel,
        out_shape=jax.ShapeDtypeStruct((ROWS, QCOLS), jnp.bfloat16),
        in_specs=[vmem, vmem, smem, vmem, vmem],
        out_specs=vmem,
        scratch_shapes=[
            pltpu.VMEM((4, 16, HDIM), jnp.bfloat16),
            pltpu.VMEM((NG, 16, HDIM), jnp.bfloat16),
            pltpu.VMEM((2, 2, NZ, 2, 2, 2, 16, LPART), jnp.bfloat16),
            pltpu.VMEM((2, 2, NZ, 2, 2, 2, 16, HDIM), jnp.bfloat16),
            pltpu.VMEM((2, 2, NZ, 2, 2, 2, 16, QPART), jnp.bfloat16),
            pltpu.VMEM((ROWS, QCOLS), jnp.bfloat16),
            pltpu.VMEM((NZ, 2, ROWS, RANK), jnp.bfloat16),
            pltpu.VMEM((NZ, 2, 8, ROWS), jnp.int32),
            pltpu.VMEM((RANK, QCOLS), jnp.bfloat16),
            pltpu.VMEM((QCOLS, RANK), jnp.bfloat16),
            pltpu.VMEM((NZ, 2 * ROWS, QCOLS), jnp.bfloat16),
            pltpu.VMEM((NZ, QCOLS, 2 * ROWS), jnp.bfloat16),
            pltpu.VMEM((HEADS, 1, ROWS), jnp.float32),
            pltpu.VMEM((HEADS, 1, ROWS), jnp.float32),
            pltpu.VMEM((HEADS, HDIM, ROWS), jnp.float32),
            dma((NG,)),
            dma((NG,)),
            dma((KINDS, NZ)),
            dma((KINDS, NZ)),
            dma((NZ,)),
            dma((NZ,)),
            dma((KINDS, 2, 4)),
            dma((KINDS, 2, 4)),
            dma,
            dma,
            dma((KINDS, 2, 4)),
            dma((KINDS, 2, 4)),
            dma((KINDS, 2, 4)),
            dma((KINDS, 2, 4)),
            dma,
            dma,
            dma((2, 8, 2)),
            dma((2, 8, 2)),
        ],
        compiler_params=pltpu.CompilerParams(
            collective_id=0, has_side_effects=True, vmem_limit_bytes=48 * 1024 * 1024
        ),
    )(
        arrivals,
        slots.reshape(1, ROWS),
        lengths,
        w_joined,
        w_expand,
    )


def solution(mesh):
    in_specs = (
        P(("group", "mp"), None),
        P(("group", "mp")),
        P("group", None),
        P("mp", "group"),
        P("mp", "group"),
    )
    out_specs = P(("group", "mp"), None)
    return jax.shard_map(body, mesh=mesh, in_specs=in_specs, out_specs=out_specs, check_vma=False)
```

```python
import functools

import jax
import jax.numpy as jnp
from jax import lax
from jax.experimental import pallas as pl
from jax.experimental.pallas import tpu as pltpu
from jax.sharding import PartitionSpec as P

HEADS = 8
HDIM = 128
QCOLS = HEADS * HDIM
RANK = 512
WIDTH = 2048
ROWS = 128
NZ = 16
NG = 16
SHARD = 96
QPART = 256
LPART = 128
KINDS = 3
TOGETHER = 8
EPS = 1e-06
NEGATIVE = -1e30
OPEN = float("inf")
MESH = pl.DeviceIdType.MESH
LAST = (((1,), (1,)), ((), ()))


def kernel(
    arrivals_ref,
    slot_row_ref,
    lengths_ref,
    joined_ref,
    expand_ref,
    out_ref,
    wide,
    shards,
    full_lat,
    full_map,
    full_query,
    query,
    lat,
    kpos,
    key_map,
    value_map,
    keys,
    values,
    peak,
    total,
    acc,
    g_send,
    g_recv,
    z_send,
    z_recv,
    kz_send,
    kz_recv,
    y_send,
    y_recv,
    ky_send,
    ky_recv,
    x_send,
    x_recv,
    c_send,
    c_recv,
    h_send,
    h_recv,
    r_send,
    r_recv,
):
    g = lax.axis_index("group")
    m = lax.axis_index("mp")
    core, x, ylo = g % 2, (g // 2) % 4, g // 8
    z, yhi = m // 2, m % 2
    xl, xh = x % 2, x // 2
    y = yhi * 2 + ylo

    def group_of(ylo_, x_, core_):
        return (ylo_ * 4 + x_) * 2 + core_

    def mp_of(z_, yhi_):
        return z_ * 2 + yhi_

    def flip(value, bits, span):
        if span == 2:
            return (value + bits) % 2
        if bits == 2:
            return (value + 2) % 4
        low = value % 2
        if bits == 1:
            return value + 1 - 2 * low
        return 3 - value

    def y_peer(k):
        other = flip(y, k, 4)
        return (group_of(other % 2, x, core), mp_of(z, other // 2))

    def x_peer(k):
        return (group_of(ylo, flip(x, k, 4), core), m)

    core_peer = (group_of(ylo, x, 1 - core), m)
    half_peer = (g, mp_of(z, 1 - yhi))
    right = (g, mp_of((z + 1) % NZ, yhi))
    left = (g, mp_of((z + NZ - 1) % NZ, yhi))

    barrier = pltpu.get_barrier_semaphore()

    def greet(peer):
        pl.semaphore_signal(barrier, inc=1, device_id=peer, device_id_type=MESH)

    def distance(index):
        return NZ // 2 + (index // 2) * (1 - 2 * (index % 2))

    @pl.loop(1, NZ)
    def _(index):
        greet((g, mp_of((z + distance(index)) % NZ, yhi)))

    @pl.loop(1, NG)
    def _(k):
        greet(((g + k) % NG, m))

    greet(y_peer(2))
    greet(y_peer(3))

    def remote(src, dst, send, recv, peer):
        return pltpu.make_async_remote_copy(
            src_ref=src,
            dst_ref=dst,
            send_sem=send,
            recv_sem=recv,
            device_id=peer,
            device_id_type=MESH,
        )

    wide[...] = jnp.zeros_like(wide)
    wide[:, :, :SHARD] = joined_ref[...].astype(jnp.bfloat16).reshape(4, 16, SHARD)
    kpos[z, yhi] = jnp.broadcast_to(slot_row_ref[...], (8, ROWS))
    rows_at = g % 4
    part = g // 4
    shards[g] = wide[rows_at]

    def placing(first, count, start, width):
        row = lax.broadcasted_iota(jnp.int32, (count * HDIM, width), 0)
        col = lax.broadcasted_iota(jnp.int32, (count * HDIM, width), 1)
        inside = row % HDIM
        same = (inside < SHARD) & ((first + row // HDIM) * SHARD + inside == start + col)
        return jnp.where(same, 1.0, 0.0).astype(jnp.bfloat16)

    def placed(first, count, start, width):
        pieces = jnp.concatenate([shards[first + t] for t in range(count)], axis=1)
        return jnp.dot(
            pieces, placing(first, count, start, width), preferred_element_type=jnp.float32
        ).astype(jnp.bfloat16)

    pl.semaphore_wait(barrier, 32)

    @pl.loop(1, NG)
    def _(k):
        other = (g + k) % NG
        remote(
            wide.at[other % 4], shards.at[g], g_send.at[k], g_recv.at[k], (other, m)
        ).start()

    @pl.loop(1, NZ)
    def _(dz):
        peer = (g, mp_of((z + dz) % NZ, yhi))
        remote(kpos.at[z, yhi], kpos.at[z, yhi], kz_send.at[dz], kz_recv.at[dz], peer).start()

    @pl.loop(1, NG)
    def _(k):
        slot = shards.at[(g + NG - k) % NG]
        remote(slot, slot, g_send.at[k], g_recv.at[k], core_peer).wait_recv()

    fulls = (full_lat, full_map, full_query)

    def z_start(kind):
        @pl.loop(1, NZ)
        def _(index):
            dz = distance(index)
            peer = (g, mp_of((z + dz) % NZ, yhi))
            mine = fulls[kind].at[ylo, xh, z, yhi, xl, core]
            remote(mine, mine, z_send.at[kind, dz], z_recv.at[kind, dz], peer).start()

    def z_wait(kind):
        @pl.loop(1, NZ)
        def _(dz):
            slot = fulls[kind].at[ylo, xh, (z + NZ - dz) % NZ, yhi, xl, core]
            remote(slot, slot, z_send.at[kind, dz], z_recv.at[kind, dz], right).wait_recv()

    lat_start = QCOLS + LPART * part
    full_lat[ylo, xh, z, yhi, xl, core] = placed(lat_start // SHARD, 2, lat_start, LPART)
    z_start(0)
    full_map[ylo, xh, z, yhi, xl, core] = expand_ref[...].astype(jnp.bfloat16)
    query_start = QPART * part
    full_query[ylo, xh, z, yhi, xl, core] = placed(query_start // SHARD, 4, query_start, QPART)

    def zs(half):
        return pl.ds(half * (NZ // 2), NZ // 2)

    def y_part(kind, half, y_, core_):
        if half == 0:
            return fulls[kind].at[y_ % 2, xh, zs(half), y_ // 2, xl, core_]
        return fulls[kind].at[y_ % 2, :, zs(half), y_ // 2, :, core_]

    def x_part(kind, half, x_, core_):
        if half == 0:
            return fulls[kind].at[:, x_ // 2, zs(half), :, x_ % 2, core_]
        return fulls[kind].at[ylo, x_ // 2, zs(half), yhi, x_ % 2, core_]

    def along(axis, kind, half, k):
        if axis == "y":
            block, peer, send, recv = y_part(kind, half, y, core), y_peer(k), y_send, y_recv
        else:
            block, peer, send, recv = x_part(kind, half, x, core), x_peer(k), x_send, x_recv
        return remote(block, block, send.at[kind, half, k], recv.at[kind, half, k], peer)

    def arrival(axis, kind, half, k):
        if axis == "y":
            block, send, recv = y_part(kind, half, flip(y, k, 4), core), y_send, y_recv
        else:
            block, send, recv = x_part(kind, half, flip(x, k, 4), core), x_send, x_recv
        return remote(block, block, send.at[kind, half, k], recv.at[kind, half, k], core_peer)

    order = (("y", "x"), ("x", "y"))

    def stage_start(kind, stage):
        for k in (2, 1, 3):
            for half in range(2):
                along(order[half][stage], kind, half, k).start()

    def stage_wait(kind, stage, half):
        for k in (1, 3, 2):
            arrival(order[half][stage], kind, half, k).wait_recv()

    def c_copy(kind, half, k, core_):
        if half == 0:
            block = x_part(kind, 0, flip(x, k, 4) if k else x, core_)
        else:
            block = y_part(kind, 1, flip(y, k, 4) if k else y, core_)
        return remote(
            block, block, c_send.at[kind, half, k], c_recv.at[kind, half, k], core_peer
        )

    def first_stage_end(kind):
        for half in range(2):
            stage_wait(kind, 0, half)
        stage_start(kind, 1)
        for half in range(2):
            c_copy(kind, half, 0, core).start()

    def second_stage_end(kind):
        for k in (1, 3, 2):
            for half in range(2):
                arrival(order[half][1], kind, half, k).wait_recv()
                c_copy(kind, half, k, core).start()

    def core_end(kind):
        for k in (0, 1, 3, 2):
            for half in range(2):
                c_copy(kind, half, k, 1 - core).wait_recv()

    rows_in = arrivals_ref[...].astype(jnp.float32)
    mean_sq = jnp.mean(rows_in * rows_in, axis=-1, keepdims=True)
    normed = (rows_in * lax.rsqrt(mean_sq + EPS)).astype(jnp.bfloat16)

    z_wait(0)
    stage_start(0, 0)
    z_start(1)
    z_start(2)
    first_stage_end(0)
    z_wait(1)
    stage_start(1, 0)

    @pl.loop(1, NZ)
    def _(dz):
        block = kpos.at[(z + NZ - dz) % NZ, yhi]
        remote(block, block, kz_send.at[dz], kz_recv.at[dz], right).wait_recv()

    key_copy = remote(kpos.at[:, yhi], kpos.at[:, yhi], ky_send, ky_recv, half_peer)
    key_copy.start()
    second_stage_end(0)
    core_end(0)

    raws = []
    for c in range(2):
        weight = jnp.concatenate(
            [full_lat[c, t].reshape(WIDTH, LPART) for t in range(2)], axis=1
        )
        raws.append(jnp.dot(normed, weight, preferred_element_type=jnp.float32))
    raw = jnp.concatenate(raws, axis=1)
    raw_sq = jnp.mean(raw * raw, axis=-1, keepdims=True)
    lat[z, yhi] = (raw * lax.rsqrt(raw_sq + EPS)).astype(jnp.bfloat16)

    def half_copy(yhi_):
        return remote(lat.at[z, yhi_], lat.at[z, yhi_], h_send, h_recv, half_peer)

    def ring_send(way, step, half):
        source = (z + NZ - step) % NZ if way == 0 else (z + step) % NZ
        block = lat.at[source, half]
        peer = right if way == 0 else left
        return remote(
            block, block, r_send.at[way, step, half], r_recv.at[way, step, half], peer
        )

    def ring_arrival(way, step, half):
        source = (z + 2 * NZ - 1 - step) % NZ if way == 0 else (z + 1 + step) % NZ
        block = lat.at[source, half]
        return remote(
            block, block, r_send.at[way, step, half], r_recv.at[way, step, half], right
        )

    half_copy(yhi).start()
    ring_send(0, 0, yhi).start()
    ring_send(1, 0, yhi).start()
    first_stage_end(1)
    z_wait(2)
    stage_start(2, 0)
    half_copy(1 - yhi).wait_recv()
    ring_send(0, 0, 1 - yhi).start()
    ring_send(1, 0, 1 - yhi).start()
    remote(kpos.at[:, 1 - yhi], kpos.at[:, 1 - yhi], ky_send, ky_recv, half_peer).wait_recv()

    def pass_on(step):
        for half in (yhi, 1 - yhi):
            for way in range(2):
                ring_arrival(way, step, half).wait_recv()
                if step < 6:
                    ring_send(way, step + 1, half).start()
        if step == 6:
            for way in range(2):
                ring_send(way, 7, way).start()

    pass_on(0)
    second_stage_end(1)
    first_stage_end(2)
    core_end(1)

    def expand_block(index):
        ylo_, x_, core_ = index // 8, (index // 2) % 4, index % 2
        return full_map[ylo_, x_ // 2, :, :, x_ % 2, core_].reshape(RANK, HDIM)

    eye_row = lax.broadcasted_iota(jnp.int32, (ROWS, ROWS), 0)
    eye_col = lax.broadcasted_iota(jnp.int32, (ROWS, ROWS), 1)
    diagonal = eye_row == eye_col
    eye = jnp.where(diagonal, 1.0, 0.0).astype(jnp.bfloat16)
    for h in range(HEADS):
        cols = slice(h * HDIM, (h + 1) * HDIM)
        key_map[:, cols] = expand_block(2 * h)
        value_map[cols, :] = lax.dot_general(
            eye, expand_block(2 * h + 1), LAST, preferred_element_type=jnp.float32
        ).astype(jnp.bfloat16)

    query_pos = slot_row_ref[...].astype(jnp.float32)
    slot_row = slot_row_ref[...]
    first = jnp.zeros_like(slot_row)
    end = lengths_ref[0, 0]
    for p in range(1, 4):
        first = jnp.where(slot_row >= end, end, first)
        end = end + lengths_ref[0, p]
    first = first.astype(jnp.float32)

    def widen(source):
        block = lat[source].reshape(2 * ROWS, RANK)
        keys[source] = jnp.dot(
            block, key_map[...], preferred_element_type=jnp.float32
        ).astype(jnp.bfloat16)
        values[source] = lax.dot_general(
            value_map[...], block, LAST, preferred_element_type=jnp.float32
        ).astype(jnp.bfloat16)

    def limit_of(source):
        limits = []
        for half in range(2):
            row = kpos[source, half][0:1].astype(jnp.float32)
            col = jnp.sum(jnp.where(diagonal, row, 0.0), axis=1, keepdims=True)
            allowed = (col <= query_pos) & (col >= first)
            limits.append(jnp.where(allowed, OPEN, NEGATIVE))
        return jnp.concatenate(limits, axis=0)

    def attend(sources, start):
        limits = [limit_of(source) for source in sources]
        def scores_of(h):
            cols = slice(h * HDIM, (h + 1) * HDIM)
            return [
                jnp.minimum(
                    lax.dot_general(
                        keys[source, :, cols],
                        query[:, cols],
                        LAST,
                        preferred_element_type=jnp.float32,
                    ),
                    limit,
                )
                for source, limit in zip(sources, limits)
            ]

        def weigh(h, scores):
            top = functools.reduce(
                jnp.maximum, [jnp.max(score, axis=0, keepdims=True) for score in scores]
            )
            if not start:
                old = peak[h]
                top = jnp.maximum(old, top)
            weights = [jnp.exp(score - top) for score in scores]
            added = sum(jnp.sum(weight, axis=0, keepdims=True) for weight in weights)
            rescale = None
            if start:
                total[h] = added
            else:
                rescale = jnp.exp(old - top)
                total[h] = total[h] * rescale + added
            peak[h] = top
            return [weight.astype(jnp.bfloat16) for weight in weights], rescale

        def gather(h, weights, rescale):
            cols = slice(h * HDIM, (h + 1) * HDIM)
            update = sum(
                jnp.dot(
                    values[source, cols, :], weight, preferred_element_type=jnp.float32
                )
                for source, weight in zip(sources, weights)
            )
            acc[h] = update if start else acc[h] * rescale + update

        for first_head in range(0, HEADS, TOGETHER):
            heads = range(first_head, first_head + TOGETHER)
            scored = [scores_of(h) for h in heads]
            weighed = [weigh(h, scores) for h, scores in zip(heads, scored)]
            for h, (weights, rescale) in zip(heads, weighed):
                gather(h, weights, rescale)

    def pair(step):
        return [(z + 2 * NZ - 1 - step) % NZ, (z + 1 + step) % NZ]

    def widen_pair(step):
        for source in pair(step):
            widen(source)

    pass_on(1)
    widen(z)
    widen_pair(0)
    pass_on(2)
    widen_pair(1)
    second_stage_end(2)
    pass_on(3)
    widen_pair(2)
    core_end(2)

    def project(c):
        weight = full_query[c // 2, c % 2].reshape(WIDTH, QPART)
        query[:, c * QPART : (c + 1) * QPART] = (
            jnp.dot(normed, weight, preferred_element_type=jnp.float32) * HDIM ** (-0.5)
        ).astype(jnp.bfloat16)

    for c in range(4):
        project(c)
    attend([z], True)
    pass_on(4)
    widen_pair(3)

    @pl.loop(0, 3)
    def _(step):
        attend(pair(step), False)

    pass_on(5)

    @pl.loop(4, 6)
    def _(step):
        widen_pair(step)
        attend(pair(step - 1), False)

    @pl.loop(1, NG)
    def _(k):
        remote(
            wide.at[(g + k) % 4], shards.at[g], g_send.at[k], g_recv.at[k], core_peer
        ).wait_send()

    @pl.loop(1, NZ)
    def _(dz):
        for kind in range(KINDS):
            mine = fulls[kind].at[ylo, xh, z, yhi, xl, core]
            remote(mine, mine, z_send.at[kind, dz], z_recv.at[kind, dz], right).wait_send()
        block = kpos.at[z, yhi]
        remote(block, block, kz_send.at[dz], kz_recv.at[dz], right).wait_send()

    key_copy.wait_send()
    for kind in range(KINDS):
        for half in range(2):
            for axis in ("x", "y"):
                for k in (1, 2, 3):
                    along(axis, kind, half, k).wait_send()
            for k in range(4):
                c_copy(kind, half, k, core).wait_send()
    half_copy(yhi).wait_send()

    @pl.loop(0, 6)
    def _(step):
        for half in range(2):
            for way in range(2):
                ring_send(way, step, half).wait_send()

    pass_on(6)
    widen_pair(6)

    @pl.loop(5, 7)
    def _(step):
        attend(pair(step), False)

    for way in range(2):
        ring_arrival(way, 7, way).wait_recv()
    widen((z + 8) % NZ)
    attend([(z + 8) % NZ], False)

    for h in range(HEADS):
        mixed = (acc[h] / total[h]).astype(jnp.bfloat16)
        out_ref[:, h * HDIM : (h + 1) * HDIM] = lax.dot_general(
            eye, mixed, LAST, preferred_element_type=jnp.float32
        ).astype(jnp.bfloat16)

    for half in range(2):
        for way in range(2):
            ring_send(way, 6, half).wait_send()
    for way in range(2):
        ring_send(way, 7, way).wait_send()


def body(arrivals, slots, lengths, w_joined, w_expand):
    vmem = pl.BlockSpec(memory_space=pltpu.VMEM)
    smem = pl.BlockSpec(memory_space=pltpu.SMEM)
    dma = pltpu.SemaphoreType.DMA
    return pl.pallas_call(
        kernel,
        out_shape=jax.ShapeDtypeStruct((ROWS, QCOLS), jnp.bfloat16),
        in_specs=[vmem, vmem, smem, vmem, vmem],
        out_specs=vmem,
        scratch_shapes=[
            pltpu.VMEM((4, 16, HDIM), jnp.bfloat16),
            pltpu.VMEM((NG, 16, HDIM), jnp.bfloat16),
            pltpu.VMEM((2, 2, NZ, 2, 2, 2, 16, LPART), jnp.bfloat16),
            pltpu.VMEM((2, 2, NZ, 2, 2, 2, 16, HDIM), jnp.bfloat16),
            pltpu.VMEM((2, 2, NZ, 2, 2, 2, 16, QPART), jnp.bfloat16),
            pltpu.VMEM((ROWS, QCOLS), jnp.bfloat16),
            pltpu.VMEM((NZ, 2, ROWS, RANK), jnp.bfloat16),
            pltpu.VMEM((NZ, 2, 8, ROWS), jnp.int32),
            pltpu.VMEM((RANK, QCOLS), jnp.bfloat16),
            pltpu.VMEM((QCOLS, RANK), jnp.bfloat16),
            pltpu.VMEM((NZ, 2 * ROWS, QCOLS), jnp.bfloat16),
            pltpu.VMEM((NZ, QCOLS, 2 * ROWS), jnp.bfloat16),
            pltpu.VMEM((HEADS, 1, ROWS), jnp.float32),
            pltpu.VMEM((HEADS, 1, ROWS), jnp.float32),
            pltpu.VMEM((HEADS, HDIM, ROWS), jnp.float32),
            dma((NG,)),
            dma((NG,)),
            dma((KINDS, NZ)),
            dma((KINDS, NZ)),
            dma((NZ,)),
            dma((NZ,)),
            dma((KINDS, 2, 4)),
            dma((KINDS, 2, 4)),
            dma,
            dma,
            dma((KINDS, 2, 4)),
            dma((KINDS, 2, 4)),
            dma((KINDS, 2, 4)),
            dma((KINDS, 2, 4)),
            dma,
            dma,
            dma((2, 8, 2)),
            dma((2, 8, 2)),
        ],
        compiler_params=pltpu.CompilerParams(
            collective_id=0, has_side_effects=True, vmem_limit_bytes=48 * 1024 * 1024
        ),
    )(
        arrivals,
        slots.reshape(1, ROWS),
        lengths,
        w_joined,
        w_expand,
    )


def solution(mesh):
    in_specs = (
        P(("group", "mp"), None),
        P(("group", "mp")),
        P("group", None),
        P("mp", "group"),
        P("mp", "group"),
    )
    out_specs = P(("group", "mp"), None)
    return jax.shard_map(body, mesh=mesh, in_specs=in_specs, out_specs=out_specs, check_vma=False)
```
